128 devices in a mesh: pipe: 4 (over z), expert: 32 (over x, y, core).
Axes of the slice: x: 4, y: 4, z: 4, core: 2. Of those that a mesh axis runs over, the one named last changes fastest.
Arguments:
- down_tokens: bfloat16 [2, 1024, 3584], P(None, 'expert'), may hold values from -6 to 6
- up_tokens: bfloat16 [2, 1024, 3584], P(None, 'expert'), may hold values from -6 to 6
- norm_gain: float32 [4, 3584], P('pipe'), may hold values from 0.1 to 1.9
- w_gate: bfloat16 [4, 32, 3584, 1024], P('pipe', 'expert'), may hold values from -0.09375 to 0.09375
- w_up: bfloat16 [4, 32, 3584, 1024], P('pipe', 'expert'), may hold values from -0.09375 to 0.09375
- w_down: bfloat16 [4, 32, 1024, 3584], P('pipe', 'expert'), may hold values from -0.1875 to 0.1875
- down_ids: int32 [4, 2, 1024, 8], P('pipe', None, 'expert'), may hold values from 0 to 31, all different within a row; in each aligned block of 32 rows (0 to 31, 32 to 63, ..., all dimensions but the last counted through in order) at most 10 rows name the same one
- down_gates: float32 [4, 2, 1024, 8], P('pipe', None, 'expert'), may hold values from 0.1 to 1
- up_ids: int32 [4, 2, 1024, 8], P('pipe', None, 'expert'), may hold values from 0 to 31, all different within a row; in each aligned block of 32 rows (0 to 31, 32 to 63, ..., all dimensions but the last counted through in order) at most 10 rows name the same one
- up_gates: float32 [4, 2, 1024, 8], P('pipe', None, 'expert'), may hold values from 0.1 to 1
- key_cotangent: bfloat16 [4, 2, 2, 1024, 64], P('pipe', None, None, 'expert'), may hold values from -0.119628906 to 0.119628906
Outputs:
- down_states: bfloat16 [4, 2, 1024, 3584], P('pipe', None, 'expert')
- up_states: bfloat16 [4, 2, 1024, 3584], P('pipe', None, 'expert')
- kr_grad: float32 [4, 3584, 64], P('pipe', 'expert')
The draws below stay inside these ranges and needn't reach their ends.
Inputs may be any that keep to these rules, and one draw needn't show every extreme that they name: `down_ids`: each row names 8 different experts. Among the 32 rows of one device in one micro-batch at one section, no expert is named more than 10 times, a bound that some block reaches. `up_ids`: each row names 8 different experts. Among the 32 rows of one device in one micro-batch at one section, no expert is named more than 10 times, a bound that some block reaches.
All inputs are finite; a program needn't handle non-finite values.
Results may differ from the reference program's by a relative error of at most 0.017.
Values may be sent and summed in bfloat16 or wider, within the bound.
No kernel may reach another device: no remote copies, remote signals or barrier semaphores. Data moves between devices by JAX's collectives and lax.ppermute only.
A program may use at most 128 MiB of HBM per device.

```python
import math
import jax
import jax.numpy as jnp
import numpy as np
from jax import lax

D = 3584
H = 1024
ROPE = 64
TOP = 8
MB = 2
TOK_DEV = 32
EXPERTS = 32
CAP = 10
TOKENS = 1024
N_PIPE = 4
N_EXPERT = 32


def level_of(own_key, shape, cuts, least, largest):
    gain = 1.0
    for dim, parts in cuts:
        heights = jax.random.uniform(jax.random.fold_in(jax.random.fold_in(own_key, 6), dim), (parts,), jnp.float32, least / len(cuts), largest / len(cuts))
        gain = gain * jnp.repeat(jnp.exp(heights), shape[dim] // parts).reshape((-1,) + (1,) * (len(shape) - 1 - dim))
    return gain


def shared_out(rng, own, number, rows, amount, top, bound, slope):
    order = jax.random.permutation(rng, amount)
    heavy_load, ordinary = shares(amount, rows * top, bound, slope, True), shares(amount, rows * top, bound, slope, False)
    places = jnp.arange(amount)

    def named(lengths, offset_by):
        used = int((lengths > 0).sum())
        fixed = max(1, used // 4)
        shifted = fixed + (places - fixed + offset_by * (used - fixed)) % max(1, amount - fixed)
        return jnp.zeros((amount,), jnp.int32).at[order[jnp.where(places < fixed, places, shifted)]].set(jnp.asarray(lengths, jnp.int32))

    lengths = jnp.where(number % 4 == 0, named(heavy_load, number // 4), named(ordinary, number - number // 4 - 1))
    mixed = jax.random.permutation(jax.random.fold_in(own, 3), amount)
    donor, sink = mixed[0:amount // 2 * 2:2], mixed[1:amount // 2 * 2:2]
    room = jnp.minimum(lengths[donor] - 1, bound - lengths[sink]) // 2
    room = jnp.where((donor == order[0]) | (sink == order[0]) | (lengths[sink] == 0), 0, jnp.maximum(room, 0))
    shifted = jax.random.randint(jax.random.fold_in(own, 4), (amount // 2,), 0, 1 << 20) % (room + 1)
    lengths = lengths.at[donor].add(-shifted).at[sink].add(shifted)
    members = jnp.searchsorted(jnp.cumsum(lengths), jnp.arange(rows * top), side="right").astype(jnp.int32)
    listing = members.reshape(top, rows).T
    listing = listing[jax.random.permutation(jax.random.fold_in(own, 1), rows)]
    offset_by = jax.random.randint(jax.random.fold_in(own, 2), (rows, 1), 0, top)
    return jnp.take_along_axis(listing, (jnp.arange(top)[None, :] + offset_by) % top, axis=1)


def shares(number_of, total, limit, skew, full):
    loads = [(1 << 20) // math.isqrt(grade ** skew) + 1 for grade in range(1, number_of + 1)]
    largest = limit if full else min(limit, max(-(-total // number_of), total * loads[0] // sum(loads)))
    least = 1 if total - largest >= number_of - 1 else 0
    given, spare = [largest] + [least] * (number_of - 1), total - largest - least * (number_of - 1)
    while spare > 0:
        movable = [i for i in range(1, number_of) if given[i] < largest] or [i for i in range(1, number_of) if given[i] < limit]
        mass, remaining = sum([loads[i] for i in movable]), spare
        for i in movable:
            addition = min(limit - given[i], max(1, remaining * loads[i] // mass), spare)
            given[i] = given[i] + addition
            spare = spare - addition
    return np.array(given)


def normal_values(stream_key, extent, spread, limit, split=(), kind=jnp.bfloat16):
    entries = jax.random.normal(stream_key, extent, jnp.float32) * spread
    if len(split) > 0:
        entries = level_of(stream_key, extent, split, -0.22, 0.18) * entries
    return jnp.clip(entries, min=-limit, max=limit).astype(kind)


def setup_inputs(seed: int = 0) -> dict:
    streams_of = jax.random.split(jax.random.key(seed), 12)
    down_tokens = normal_values(streams_of[0], (MB, TOKENS, D), 1.0, 6.0, ((1, 32),))
    up_tokens = normal_values(streams_of[1], (MB, TOKENS, D), 1.0, 6.0, ((1, 32),))
    norm_gain = jnp.clip(1.0 + 0.18 * jax.random.normal(streams_of[2], (N_PIPE, D), jnp.float32), 0.1, 1.9)
    w_gate = normal_values(streams_of[3], (N_PIPE, EXPERTS, D, H), D ** -0.5, 0.09375, ((0, 4), (1, 32)))
    w_up = normal_values(streams_of[4], (N_PIPE, EXPERTS, D, H), D ** -0.5, 0.09375, ((0, 4), (1, 32)))
    w_down = normal_values(streams_of[5], (N_PIPE, EXPERTS, H, D), H ** -0.5, 0.1875, ((0, 4), (1, 32)))
    down_ids_keys = jax.random.split(jax.random.fold_in(streams_of[6], 1), N_PIPE * MB * TOKENS // TOK_DEV)
    down_ids_turns = jax.random.permutation(jax.random.fold_in(streams_of[6], 3), N_PIPE * MB * TOKENS // TOK_DEV)
    down_ids = jax.vmap(lambda own, number: shared_out(jax.random.fold_in(streams_of[6], 2), own, number, TOK_DEV, EXPERTS, TOP, CAP, 1))(down_ids_keys, down_ids_turns).reshape((N_PIPE, MB, TOKENS, TOP))
    down_gates = jnp.clip(jnp.exp(math.log(1.0) - 2.3025851 * jax.random.uniform(streams_of[7], (N_PIPE, MB, TOKENS, TOP), jnp.float32) ** level_of(streams_of[7], (N_PIPE, MB, TOKENS, TOP), ((0, 4), (2, 32)), -0.2, 0.2)), 0.1, 1.0)
    up_ids_keys = jax.random.split(jax.random.fold_in(streams_of[8], 1), N_PIPE * MB * TOKENS // TOK_DEV)
    up_ids_turns = jax.random.permutation(jax.random.fold_in(streams_of[8], 3), N_PIPE * MB * TOKENS // TOK_DEV)
    up_ids = jax.vmap(lambda own, number: shared_out(jax.random.fold_in(streams_of[8], 2), own, number, TOK_DEV, EXPERTS, TOP, CAP, 1))(up_ids_keys, up_ids_turns).reshape((N_PIPE, MB, TOKENS, TOP))
    up_gates = jnp.clip(jnp.exp(math.log(1.0) - 2.3025851 * jax.random.uniform(streams_of[9], (N_PIPE, MB, TOKENS, TOP), jnp.float32) ** level_of(streams_of[9], (N_PIPE, MB, TOKENS, TOP), ((0, 4), (2, 32)), -0.2, 0.2)), 0.1, 1.0)
    key_cotangent = normal_values(streams_of[10], (N_PIPE, 2, MB, TOKENS, ROPE), 0.02, 0.119628906, ((0, 4), (3, 32)))
    return {"down_tokens": down_tokens, "up_tokens": up_tokens, "norm_gain": norm_gain, "w_gate": w_gate, "w_up": w_up, "w_down": w_down, "down_ids": down_ids, "down_gates": down_gates, "up_ids": up_ids, "up_gates": up_gates, "key_cotangent": key_cotangent}


EPSILON = 1e-06

def normalize(carried, norm_scale):
    values = carried.astype(jnp.float32)
    inv_rms = lax.rsqrt(lax.optimization_barrier(jnp.mean(values * values, axis=-1, keepdims=True)) + EPSILON)
    return (values * inv_rms * norm_scale).astype(jnp.bfloat16)

def expert_rows(row_block, gate_mat, up_mat, down_mat):
    gate_act = jnp.dot(row_block, gate_mat, preferred_element_type=jnp.float32)
    up_act = jnp.dot(row_block, up_mat, preferred_element_type=jnp.float32)
    hidden = (jax.nn.silu(gate_act) * up_act).astype(jnp.bfloat16)
    return jnp.dot(hidden, down_mat, preferred_element_type=jnp.float32).astype(jnp.bfloat16)

def moe_layer(carried, norm_scale, gate_all, up_all, down_all, route_ids, route_gates):
    normed = normalize(carried, norm_scale)
    flat_ids = route_ids.reshape(-1).astype(jnp.int32)
    flat_gates = route_gates.reshape(-1).astype(jnp.float32)
    row_limit = N_EXPERT * CAP
    positions = jnp.arange(row_limit, dtype=jnp.int32)

    def per_expert(accum, expert):
        matched = flat_ids == expert
        live_count = jnp.sum(matched.astype(jnp.int32))
        pick_index = jnp.nonzero(matched, size=row_limit, fill_value=0)[0].astype(jnp.int32)
        token_index = (pick_index // TOP).astype(jnp.int32)
        outputs = expert_rows(normed[token_index], gate_all[expert], up_all[expert], down_all[expert])
        pick_weight = jnp.where(positions < live_count, flat_gates[pick_index], jnp.zeros_like(flat_gates[pick_index]))
        contrib = pick_weight[:, None] * outputs.astype(jnp.float32)
        return (accum.at[token_index].add(contrib), None)
    accum_start = jnp.zeros(carried.shape, jnp.float32)
    accum, unused = lax.scan(per_expert, accum_start, jnp.arange(EXPERTS, dtype=jnp.int32))
    return ((carried.astype(jnp.float32) + accum).astype(jnp.bfloat16), normed)

def reference(down_tokens, up_tokens, norm_gain, w_gate, w_up, w_down, down_ids, down_gates, up_ids, up_gates, key_cotangent):
    down_rows = [[None] * MB for segment_index in range(N_PIPE)]
    up_rows = [[None] * MB for segment_index in range(N_PIPE)]
    grad_list = [jnp.zeros((D, ROPE), jnp.float32) for segment_index in range(N_PIPE)]
    for micro_index in range(MB):
        carried = down_tokens[micro_index]
        for segment_index in range(N_PIPE):
            carried, normed = moe_layer(carried, norm_gain[segment_index], w_gate[segment_index], w_up[segment_index], w_down[segment_index], down_ids[segment_index, micro_index], down_gates[segment_index, micro_index])
            down_rows[segment_index][micro_index] = carried
            grad_list[segment_index] = grad_list[segment_index] + jnp.dot(normed.T, key_cotangent[segment_index, 0, micro_index], preferred_element_type=jnp.float32)
        carried = up_tokens[micro_index]
        for segment_index in reversed(range(N_PIPE)):
            carried, normed = moe_layer(carried, norm_gain[segment_index], w_gate[segment_index], w_up[segment_index], w_down[segment_index], up_ids[segment_index, micro_index], up_gates[segment_index, micro_index])
            up_rows[segment_index][micro_index] = carried
            grad_list[segment_index] = grad_list[segment_index] + jnp.dot(normed.T, key_cotangent[segment_index, 1, micro_index], preferred_element_type=jnp.float32)
    down_states = jnp.stack([jnp.stack(row_list) for row_list in down_rows])
    up_states = jnp.stack([jnp.stack(row_list) for row_list in up_rows])
    return (down_states, up_states, jnp.stack(grad_list))
```

```python
from functools import partial

import jax
import jax.numpy as jnp
from jax import lax
from jax.sharding import PartitionSpec as P

EPSILON = 1e-06


def passed_along(value, axis, steps):
    count = lax.axis_size(axis)
    first, last = (max(0, -steps), min(count, count - steps))
    return lax.ppermute(value, axis, [(source, source + steps) for source in range(first, last)])


def normalize(carried, norm_scale):
    values = carried.astype(jnp.float32)
    inv_rms = lax.rsqrt(jnp.mean(values * values, axis=-1, keepdims=True) + EPSILON)
    return (values * inv_rms * norm_scale).astype(jnp.bfloat16)


def expert_rows(row_block, gate_mat, up_mat, down_mat):
    gate_act = jnp.dot(row_block, gate_mat, preferred_element_type=jnp.float32)
    up_act = jnp.dot(row_block, up_mat, preferred_element_type=jnp.float32)
    hidden = (jax.nn.silu(gate_act) * up_act).astype(jnp.bfloat16)
    return jnp.dot(hidden, down_mat, preferred_element_type=jnp.float32).astype(jnp.bfloat16)


def apply_expert(row_block, weights):
    return expert_rows(row_block, weights[0], weights[1], weights[2])


def slot_layout(route_ids, expert_count, capacity):
    expert_axis = jnp.arange(expert_count, dtype=jnp.int32)
    chosen = jnp.sum((route_ids[:, :, None] == expert_axis).astype(jnp.int32), axis=1)
    slot_rank = jnp.cumsum(chosen, axis=0) - 1
    slot_axis = jnp.arange(capacity, dtype=jnp.int32)
    return chosen[:, :, None] * (slot_rank[:, :, None] == slot_axis).astype(jnp.int32)


def run_layer(carried, norm_scale, weights, route_ids, route_gates, active):
    normed = normalize(carried, norm_scale)
    expert_count = lax.axis_size("expert")
    token_count, pick_count = route_ids.shape
    capacity = min(token_count, 5 * token_count * pick_count // (4 * expert_count))
    slot_table = slot_layout(route_ids, expert_count, capacity)
    outgoing = jnp.einsum(
        "tec,td->ecd", slot_table.astype(jnp.bfloat16), normed, preferred_element_type=jnp.float32
    ).astype(jnp.bfloat16)
    arrived = lax.all_to_all(outgoing, "expert", split_axis=0, concat_axis=0, tiled=True)
    source_count, item_count, feature_count = arrived.shape
    row_block = arrived.reshape(source_count * item_count, feature_count)
    finished = lax.cond(active, partial(apply_expert, weights=weights), jnp.zeros_like, row_block)
    returned = lax.all_to_all(
        finished.reshape(source_count, item_count, feature_count),
        "expert",
        split_axis=0,
        concat_axis=0,
        tiled=True,
    )
    expert_axis = jnp.arange(expert_count, dtype=jnp.int32)
    gate_weight = jnp.sum(
        route_gates[:, :, None] * (route_ids[:, :, None] == expert_axis).astype(jnp.float32), axis=1
    )
    weighted = (slot_table.astype(jnp.float32) * gate_weight[:, :, None]).reshape(
        token_count, expert_count * capacity
    )
    flat_returned = returned.reshape(expert_count * capacity, returned.shape[2]).astype(jnp.float32)
    combined = jnp.dot(weighted, flat_returned, precision=lax.Precision.HIGHEST)
    output = (carried.astype(jnp.float32) + combined).astype(jnp.bfloat16)
    return (output, normed)


def pass_on(values):
    to_next = passed_along(values, "pipe", 1)
    behind = passed_along(values, "pipe", -1)
    return (to_next, behind)


def grad_term(row_source, tangents):
    return jnp.einsum("td,tr->dr", row_source, tangents, preferred_element_type=jnp.float32)


def summed_grad(partial_grad, expert_count, own_rows):
    rope_width = partial_grad.shape[1]
    halves = partial_grad.reshape(expert_count, 2, own_rows // 2, rope_width)
    paired = jnp.concatenate([halves[:, 0], halves[:, 1]], axis=-1).astype(jnp.bfloat16)
    gathered = lax.all_to_all(paired, "expert", split_axis=0, concat_axis=0, tiled=True)
    total = jnp.sum(gathered.astype(jnp.float32), axis=0)
    return jnp.concatenate([total[:, :rope_width], total[:, rope_width:]], axis=0)


def on_device(
    down_tokens,
    up_tokens,
    norm_gain,
    w_gate,
    w_up,
    w_down,
    down_ids,
    down_gates,
    up_ids,
    up_gates,
    key_cotangent,
):
    segment_count = lax.axis_size("pipe")
    expert_count = lax.axis_size("expert")
    segment_pos = lax.axis_index("pipe")
    micro_count = down_tokens.shape[0]
    feature_count = down_tokens.shape[2]
    own_rows = feature_count // expert_count
    norm_scale = norm_gain[0]
    weights = (w_gate[0, 0], w_up[0, 0], w_down[0, 0])
    total_steps = segment_count + 2 * micro_count - 2
    from_prior = jnp.zeros_like(down_tokens[0])
    from_next = jnp.zeros_like(up_tokens[0])
    down_states = jnp.zeros_like(down_tokens)
    up_states = jnp.zeros_like(up_tokens)
    normed_rows = []
    tangent_rows = []
    micro_slots = jnp.arange(micro_count, dtype=jnp.int32)
    for step_index in range(total_steps):
        lag_down = step_index - segment_pos
        lag_up = step_index - (segment_count - 1 - segment_pos)
        down_on = (lag_down >= 0) & (lag_down % 2 == 0) & (lag_down < 2 * micro_count)
        up_on = (lag_up >= 0) & (lag_up % 2 == 0) & (lag_up < 2 * micro_count)
        down_mb = jnp.clip(lag_down // 2, 0, micro_count - 1)
        up_mb = jnp.clip(lag_up // 2, 0, micro_count - 1)
        down_in = jnp.where(segment_pos == 0, down_tokens[down_mb], from_prior)
        up_in = jnp.where(segment_pos == segment_count - 1, up_tokens[up_mb], from_next)
        carried = jnp.where(down_on, down_in, up_in)
        route_ids = jnp.where(down_on, down_ids[0, down_mb], up_ids[0, up_mb])
        route_gates = jnp.where(down_on, down_gates[0, down_mb], up_gates[0, up_mb])
        active = down_on | up_on
        output, normed = run_layer(carried, norm_scale, weights, route_ids, route_gates, active)
        down_states = jnp.where(
            (micro_slots == down_mb)[:, None, None] & down_on, output[None], down_states
        )
        up_states = jnp.where(
            (micro_slots == up_mb)[:, None, None] & up_on, output[None], up_states
        )
        tangent = jnp.where(down_on, key_cotangent[0, 0, down_mb], key_cotangent[0, 1, up_mb])
        tangent = tangent * active.astype(tangent.dtype)
        normed_rows.append(normed)
        tangent_rows.append(tangent)
        if step_index + 1 < total_steps:
            from_prior, from_next = pass_on(output)
    key_grad = summed_grad(
        grad_term(jnp.concatenate(normed_rows), jnp.concatenate(tangent_rows)), expert_count, own_rows
    )
    return (down_states[None], up_states[None], key_grad[None])


def solution(mesh):
    return jax.shard_map(
        on_device,
        mesh=mesh,
        in_specs=(
            P(None, "expert", None),
            P(None, "expert", None),
            P("pipe", None),
            P("pipe", "expert", None, None),
            P("pipe", "expert", None, None),
            P("pipe", "expert", None, None),
            P("pipe", None, "expert", None),
            P("pipe", None, "expert", None),
            P("pipe", None, "expert", None),
            P("pipe", None, "expert", None),
            P("pipe", None, None, "expert", None),
        ),
        out_specs=(
            P("pipe", None, "expert", None),
            P("pipe", None, "expert", None),
            P("pipe", "expert", None),
        ),
        check_vma=False,
    )
```

```python
from functools import partial

import jax
import jax.numpy as jnp
from jax import lax
from jax.experimental import pallas as pl
from jax.experimental.pallas import tpu as pltpu
from jax.sharding import PartitionSpec as P

EPSILON = 1e-06
SIDE = 4
CAP = 10
TARGETS = 2 * SIDE
MIB = 1 << 20


def device_at(x, y, core):
    return (x % SIDE) * 2 * SIDE + (y % SIDE) * 2 + core


def first_line(shift):
    pairs = []
    for x in range(SIDE):
        for y in range(SIDE):
            pairs.append((device_at(x, y, 0), device_at(x + shift, y, 0)))
            pairs.append((device_at(x, y, 1), device_at(x, y + shift, 1)))
    return pairs


def second_line(shift, flip):
    pairs = []
    for x in range(SIDE):
        for y in range(SIDE):
            pairs.append((device_at(x, y, 0), device_at(x, y + shift, flip)))
            pairs.append((device_at(x, y, 1), device_at(x + shift, y, 1 - flip)))
    return pairs


def backwards(pairs):
    return [(target, source) for source, target in pairs]


HOPS = [(shift, flip) for shift in range(SIDE) for flip in range(2)]


def along_first(blocks, back=False):
    moved = []
    for shift, block in enumerate(blocks):
        pairs = first_line(shift)
        moved.append(
            lax.ppermute(block, "expert", backwards(pairs) if back else pairs) if shift else block
        )
    return moved


def along_second(blocks, back=False):
    moved = []
    for (shift, flip), block in zip(HOPS, blocks):
        pairs = second_line(shift, flip)
        stays = shift == 0 and flip == 0
        moved.append(
            block if stays else lax.ppermute(block, "expert", backwards(pairs) if back else pairs)
        )
    return moved


def normalize(carried, norm_scale):
    values = carried.astype(jnp.float32)
    inv_rms = lax.rsqrt(jnp.mean(values * values, axis=-1, keepdims=True) + EPSILON)
    return (values * inv_rms * norm_scale).astype(jnp.bfloat16)


def routing_tables(route_ids, route_gates):
    block_count, token_count, pick_count = route_ids.shape
    packed = jnp.concatenate(
        [jnp.swapaxes(route_ids, 1, 2).astype(jnp.float32), jnp.swapaxes(route_gates, 1, 2)], axis=1
    )
    gathered = jnp.concatenate(along_first([packed] * SIDE), axis=-1)
    ids, gates = (gathered[:, :pick_count], gathered[:, pick_count:])
    position = lax.axis_index("expert")
    x, y, core = (position // (2 * SIDE), (position // 2) % SIDE, position % 2)
    shift = jnp.arange(TARGETS, dtype=jnp.int32) // 2
    flip = jnp.arange(TARGETS, dtype=jnp.int32) % 2
    experts = jnp.where(
        core == 0,
        x * 2 * SIDE + ((y + shift) % SIDE) * 2 + flip,
        ((x + shift) % SIDE) * 2 * SIDE + y * 2 + 1 - flip,
    ).astype(jnp.float32)
    matches = (ids[:, None] == experts[None, :, None, None]).astype(jnp.float32)
    chosen = jnp.sum(matches, axis=2)
    gate_of = jnp.sum(matches * gates[:, None], axis=2)
    lane = jnp.arange(SIDE * token_count, dtype=jnp.int32)
    earlier = (lane[:, None] // token_count == lane[None, :] // token_count) & (
        lane[:, None] < lane[None, :]
    )
    rank = jnp.einsum(
        "bet,tu->beu",
        chosen.astype(jnp.bfloat16),
        earlier.astype(jnp.bfloat16),
        preferred_element_type=jnp.float32,
    )
    return jnp.where(chosen > 0, rank, -1.0), gate_of


def slot_pattern(line_count, token_count):
    rows, columns = (line_count * CAP, line_count * token_count)
    row = lax.broadcasted_iota(jnp.int32, (rows, columns), 0)
    column = lax.broadcasted_iota(jnp.int32, (rows, columns), 1)
    return jnp.where(row // CAP == column // token_count, row % CAP, -2).astype(jnp.float32)


def pick_body(slots_ref, *refs):
    row_refs, out_refs = (refs[:SIDE], refs[SIDE:])
    token_count = row_refs[0].shape[0]
    pattern = slot_pattern(SIDE, token_count)
    table = jnp.concatenate(
        [(slots_ref[e : e + 1, :] == pattern).astype(jnp.float32) for e in range(TARGETS)], axis=0
    ).astype(jnp.bfloat16)
    rows = jnp.concatenate([ref[...] for ref in row_refs], axis=0)
    picked = jnp.dot(table, rows, preferred_element_type=jnp.float32)
    count = SIDE * CAP
    for e, ref in enumerate(out_refs):
        ref[...] = picked[e * count : (e + 1) * count].astype(jnp.bfloat16)


def pick_rows(slots, rows, block=512):
    token_count, features = rows[0].shape
    table_spec = pl.BlockSpec(slots.shape, lambda i: (0, 0))
    out = jax.ShapeDtypeStruct((SIDE * CAP, features), jnp.bfloat16)
    return pl.pallas_call(
        pick_body,
        name="pick_rows",
        grid=(features // block,),
        out_shape=(out,) * TARGETS,
        in_specs=[table_spec] + [pl.BlockSpec((token_count, block), lambda i: (0, i))] * SIDE,
        out_specs=(pl.BlockSpec((SIDE * CAP, block), lambda i: (0, i)),) * TARGETS,
        compiler_params=pltpu.CompilerParams(vmem_limit_bytes=32 * MIB),
    )(slots, *rows)


def merge_body(slots_ref, gates_ref, *refs):
    row_refs, out_refs = (refs[:TARGETS], refs[TARGETS:])
    token_count = out_refs[0].shape[0]
    pattern = slot_pattern(SIDE, token_count)
    weights = jnp.concatenate(
        [
            jnp.where(slots_ref[e : e + 1, :] == pattern, gates_ref[e : e + 1, :], 0.0)
            for e in range(TARGETS)
        ],
        axis=0,
    )
    rows = jnp.concatenate([ref[...].astype(jnp.float32) for ref in row_refs], axis=0)
    merged = jnp.dot(
        weights.T.astype(jnp.bfloat16),
        rows.astype(jnp.bfloat16),
        preferred_element_type=jnp.float32,
    )
    for m, ref in enumerate(out_refs):
        ref[...] = merged[m * token_count : (m + 1) * token_count].astype(jnp.bfloat16)


def merge_rows(slots, gates, rows, token_count, block=512):
    features = rows[0].shape[1]
    table_spec = pl.BlockSpec(slots.shape, lambda i: (0, 0))
    out = jax.ShapeDtypeStruct((token_count, features), jnp.bfloat16)
    return pl.pallas_call(
        merge_body,
        name="merge_rows",
        grid=(features // block,),
        out_shape=(out,) * SIDE,
        in_specs=[table_spec] * 2
        + [pl.BlockSpec((SIDE * CAP, block), lambda i: (0, i))] * TARGETS,
        out_specs=(pl.BlockSpec((token_count, block), lambda i: (0, i)),) * SIDE,
        compiler_params=pltpu.CompilerParams(vmem_limit_bytes=32 * MIB),
    )(slots, gates, *rows)


def expert_body(gate_ref, up_ref, down_ref, *refs):
    row_refs, out_refs = (refs[:TARGETS], refs[TARGETS : 2 * TARGETS])
    rows_scratch, sum_scratch = refs[2 * TARGETS :]
    step = pl.program_id(0)
    count = SIDE * CAP

    @pl.when(step == 0)
    def _():
        rows_scratch[...] = jnp.concatenate(
            [ref[...].astype(jnp.float32) for ref in row_refs], axis=0
        ).astype(jnp.bfloat16)

    rows = rows_scratch[...]
    gate_act = jnp.dot(rows, gate_ref[...], preferred_element_type=jnp.float32)
    up_act = jnp.dot(rows, up_ref[...], preferred_element_type=jnp.float32)
    hidden = (jax.nn.silu(gate_act) * up_act).astype(jnp.bfloat16)
    part = jnp.dot(hidden, down_ref[...], preferred_element_type=jnp.float32)

    @pl.when(step == 0)
    def _():
        sum_scratch[...] = part

    @pl.when(step > 0)
    def _():
        sum_scratch[...] += part

    @pl.when(step == pl.num_programs(0) - 1)
    def _():
        for e, ref in enumerate(out_refs):
            ref[...] = sum_scratch[e * count : (e + 1) * count, :].astype(jnp.bfloat16)


def expert_rows(rows, weights, block=256):
    gate_mat, up_mat, down_mat = weights
    features, hidden_count = gate_mat.shape
    count = SIDE * CAP
    row_spec = pl.BlockSpec((count, features), lambda i: (0, 0))
    out = jax.ShapeDtypeStruct((count, features), jnp.bfloat16)
    return pl.pallas_call(
        expert_body,
        name="expert_rows",
        grid=(hidden_count // block,),
        out_shape=(out,) * TARGETS,
        in_specs=[
            pl.BlockSpec((features, block), lambda i: (0, i)),
            pl.BlockSpec((features, block), lambda i: (0, i)),
            pl.BlockSpec((block, features), lambda i: (i, 0)),
        ]
        + [row_spec] * TARGETS,
        out_specs=(row_spec,) * TARGETS,
        scratch_shapes=[
            pltpu.VMEM((TARGETS * count, features), jnp.bfloat16),
            pltpu.VMEM((TARGETS * count, features), jnp.float32),
        ],
        compiler_params=pltpu.CompilerParams(vmem_limit_bytes=50 * MIB),
    )(gate_mat, up_mat, down_mat, *rows)


def run_layer(carried, norm_scale, weights, slots, gates):
    normed = normalize(carried, norm_scale)
    line_rows = along_first([normed] * SIDE)
    sent = pick_rows(slots, line_rows)
    arrived = along_second(sent)
    finished = expert_rows(arrived, weights)
    returned = along_second(finished, back=True)
    partial_sums = merge_rows(slots, gates, returned, carried.shape[0])
    own_sums = along_first(partial_sums, back=True)
    total = carried.astype(jnp.float32)
    for own_sum in own_sums:
        total = total + own_sum.astype(jnp.float32)
    return (total.astype(jnp.bfloat16), normed)


def summed_grad(normed, tangents):
    expert_count = lax.axis_size("expert")
    partial_grad = jnp.einsum("td,tr->dr", normed, tangents, preferred_element_type=jnp.float32)
    feature_count, rope_width = partial_grad.shape
    own_rows = feature_count // expert_count
    halves = partial_grad.reshape(expert_count, 2, own_rows // 2, rope_width)
    paired = jnp.concatenate([halves[:, 0], halves[:, 1]], axis=-1).astype(jnp.bfloat16)
    gathered = lax.all_to_all(paired, "expert", split_axis=0, concat_axis=0, tiled=True)
    total = jnp.sum(gathered.astype(jnp.float32), axis=0)
    return jnp.concatenate([total[:, :rope_width], total[:, rope_width:]], axis=0)


def on_device(
    down_tokens,
    up_tokens,
    norm_gain,
    w_gate,
    w_up,
    w_down,
    down_ids,
    down_gates,
    up_ids,
    up_gates,
    key_cotangent,
):
    segment_count = lax.axis_size("pipe")
    segment_pos = lax.axis_index("pipe")
    micro_count = down_tokens.shape[0]
    norm_scale = norm_gain[0]
    weights = (w_gate[0, 0], w_up[0, 0], w_down[0, 0])
    down_first = segment_pos < segment_count // 2
    first_step = jnp.minimum(segment_pos, segment_count - 1 - segment_pos)
    slots, gates = routing_tables(
        jnp.concatenate(
            [jnp.where(down_first, down_ids[0], up_ids[0]), jnp.where(down_first, up_ids[0], down_ids[0])]
        ),
        jnp.concatenate(
            [
                jnp.where(down_first, down_gates[0], up_gates[0]),
                jnp.where(down_first, up_gates[0], down_gates[0]),
            ]
        ),
    )
    carried = [
        jnp.where(segment_pos == 0, down_tokens[micro], up_tokens[micro])
        for micro in range(micro_count)
    ]
    outputs = {}
    normed_rows = {}
    for step in range(segment_count):
        turn = step // (segment_count // 2)
        for micro in range(micro_count):
            table = turn * micro_count + micro
            output, normed = run_layer(
                carried[micro], norm_scale, weights, slots[table], gates[table]
            )
            outputs[step, micro] = output
            normed_rows[step, micro] = normed
            if step + 1 < segment_count:
                carried[micro] = lax.ppermute(
                    output,
                    "pipe",
                    [(step, step + 1), (segment_count - 1 - step, segment_count - 2 - step)],
                )

    def turns(values):
        half = segment_count // 2
        chosen = []
        for turn in range(2):
            for micro in range(micro_count):
                value = values[turn * half, micro]
                for offset in range(1, half):
                    step = turn * half + offset
                    here = (first_step if turn == 0 else segment_count - 1 - first_step) == step
                    value = jnp.where(here, values[step, micro], value)
                chosen.append(value)
        return chosen

    turn_outputs = turns(outputs)
    first, second = (jnp.stack(turn_outputs[:micro_count]), jnp.stack(turn_outputs[micro_count:]))
    down_states = jnp.where(down_first, first, second)
    up_states = jnp.where(down_first, second, first)
    down_tangents = key_cotangent[0, 0].reshape(-1, key_cotangent.shape[-1])
    up_tangents = key_cotangent[0, 1].reshape(-1, key_cotangent.shape[-1])
    tangents = jnp.concatenate(
        [
            jnp.where(down_first, down_tangents, up_tangents),
            jnp.where(down_first, up_tangents, down_tangents),
        ]
    )
    key_grad = summed_grad(jnp.concatenate(turns(normed_rows)), tangents)
    return (down_states[None], up_states[None], key_grad[None])


def solution(mesh):
    return jax.shard_map(
        on_device,
        mesh=mesh,
        in_specs=(
            P(None, "expert", None),
            P(None, "expert", None),
            P("pipe", None),
            P("pipe", "expert", None, None),
            P("pipe", "expert", None, None),
            P("pipe", "expert", None, None),
            P("pipe", None, "expert", None),
            P("pipe", None, "expert", None),
            P("pipe", None, "expert", None),
            P("pipe", None, "expert", None),
            P("pipe", None, None, "expert", None),
        ),
        out_specs=(
            P("pipe", None, "expert", None),
            P("pipe", None, "expert", None),
            P("pipe", "expert", None),
        ),
        check_vma=False,
    )
```

```python
from functools import partial

import jax
import jax.numpy as jnp
from jax import lax
from jax.experimental import pallas as pl
from jax.experimental.pallas import tpu as pltpu
from jax.sharding import PartitionSpec as P

EPSILON = 1e-06
UNTOUCHED = pl.BlockSpec(memory_space=pl.ANY)
SIDE = 4
CAP = 10
TARGETS = 2 * SIDE
MIB = 1 << 20


def device_at(x, y, core):
    return (x % SIDE) * 2 * SIDE + (y % SIDE) * 2 + core


def first_line(shift):
    pairs = []
    for x in range(SIDE):
        for y in range(SIDE):
            pairs.append((device_at(x, y, 0), device_at(x + shift, y, 0)))
            pairs.append((device_at(x, y, 1), device_at(x, y + shift, 1)))
    return pairs


def second_line(shift, flip):
    pairs = []
    for x in range(SIDE):
        for y in range(SIDE):
            pairs.append((device_at(x, y, 0), device_at(x, y + shift, flip)))
            pairs.append((device_at(x, y, 1), device_at(x + shift, y, 1 - flip)))
    return pairs


def backwards(pairs):
    return [(target, source) for source, target in pairs]


HOPS = [(shift, flip) for shift in range(SIDE) for flip in range(2)]


def along_first(blocks, back=False):
    moved = []
    for shift, block in enumerate(blocks):
        pairs = first_line(shift)
        moved.append(
            lax.ppermute(block, "expert", backwards(pairs) if back else pairs) if shift else block
        )
    return moved


def along_second(blocks, back=False):
    moved = []
    for (shift, flip), block in zip(HOPS, blocks):
        pairs = second_line(shift, flip)
        stays = shift == 0 and flip == 0
        moved.append(
            block if stays else lax.ppermute(block, "expert", backwards(pairs) if back else pairs)
        )
    return moved


def normalize(carried, norm_scale):
    values = carried.astype(jnp.float32)
    inv_rms = lax.rsqrt(jnp.mean(values * values, axis=-1, keepdims=True) + EPSILON)
    return (values * inv_rms * norm_scale).astype(jnp.bfloat16)


def routing_tables(route_ids, route_gates):
    block_count, token_count, pick_count = route_ids.shape
    packed = jnp.concatenate(
        [jnp.swapaxes(route_ids, 1, 2).astype(jnp.float32), jnp.swapaxes(route_gates, 1, 2)], axis=1
    )
    gathered = jnp.concatenate(along_first([packed] * SIDE), axis=-1)
    ids, gates = (gathered[:, :pick_count], gathered[:, pick_count:])
    position = lax.axis_index("expert")
    x, y, core = (position // (2 * SIDE), (position // 2) % SIDE, position % 2)
    shift = jnp.arange(TARGETS, dtype=jnp.int32) // 2
    flip = jnp.arange(TARGETS, dtype=jnp.int32) % 2
    experts = jnp.where(
        core == 0,
        x * 2 * SIDE + ((y + shift) % SIDE) * 2 + flip,
        ((x + shift) % SIDE) * 2 * SIDE + y * 2 + 1 - flip,
    ).astype(jnp.float32)
    matches = (ids[:, None] == experts[None, :, None, None]).astype(jnp.float32)
    chosen = jnp.sum(matches, axis=2)
    gate_of = jnp.sum(matches * gates[:, None], axis=2)
    lane = jnp.arange(SIDE * token_count, dtype=jnp.int32)
    earlier = (lane[:, None] // token_count == lane[None, :] // token_count) & (
        lane[:, None] < lane[None, :]
    )
    rank = jnp.einsum(
        "bet,tu->beu",
        chosen.astype(jnp.bfloat16),
        earlier.astype(jnp.bfloat16),
        preferred_element_type=jnp.float32,
    )
    return jnp.where(chosen > 0, rank, -1.0), gate_of


def slot_pattern(line_count, token_count):
    rows, columns = (line_count * CAP, line_count * token_count)
    row = lax.broadcasted_iota(jnp.int32, (rows, columns), 0)
    column = lax.broadcasted_iota(jnp.int32, (rows, columns), 1)
    return jnp.where(row // CAP == column // token_count, row % CAP, -2).astype(jnp.float32)


def pick_body(slots_ref, *refs):
    row_refs, out_refs = (refs[:SIDE], refs[-TARGETS:])
    token_count = row_refs[0].shape[0]
    pattern = slot_pattern(SIDE, token_count)
    table = jnp.concatenate(
        [(slots_ref[e : e + 1, :] == pattern).astype(jnp.float32) for e in range(TARGETS)], axis=0
    ).astype(jnp.bfloat16)
    rows = jnp.concatenate([ref[...] for ref in row_refs], axis=0)
    picked = jnp.dot(table, rows, preferred_element_type=jnp.float32)
    count = SIDE * CAP
    for e, ref in enumerate(out_refs):
        ref[...] = picked[e * count : (e + 1) * count].astype(jnp.bfloat16)


def pick_rows(slots, rows, after=(), block=512):
    token_count, features = rows[0].shape
    table_spec = pl.BlockSpec(slots.shape, lambda i: (0, 0))
    out = jax.ShapeDtypeStruct((SIDE * CAP, features), jnp.bfloat16)
    return pl.pallas_call(
        pick_body,
        name="pick_rows",
        grid=(features // block,),
        out_shape=(out,) * TARGETS,
        in_specs=[table_spec]
        + [pl.BlockSpec((token_count, block), lambda i: (0, i))] * SIDE
        + [UNTOUCHED] * len(after),
        out_specs=(pl.BlockSpec((SIDE * CAP, block), lambda i: (0, i)),) * TARGETS,
        compiler_params=pltpu.CompilerParams(vmem_limit_bytes=32 * MIB),
    )(slots, *rows, *after)


def merge_body(slots_ref, gates_ref, *refs):
    row_refs, out_refs = (refs[:TARGETS], refs[-SIDE:])
    token_count = out_refs[0].shape[0]
    pattern = slot_pattern(SIDE, token_count)
    weights = jnp.concatenate(
        [
            jnp.where(slots_ref[e : e + 1, :] == pattern, gates_ref[e : e + 1, :], 0.0)
            for e in range(TARGETS)
        ],
        axis=0,
    )
    rows = jnp.concatenate([ref[...].astype(jnp.float32) for ref in row_refs], axis=0)
    merged = jnp.dot(
        weights.T.astype(jnp.bfloat16),
        rows.astype(jnp.bfloat16),
        preferred_element_type=jnp.float32,
    )
    for m, ref in enumerate(out_refs):
        ref[...] = merged[m * token_count : (m + 1) * token_count].astype(jnp.bfloat16)


def merge_rows(slots, gates, rows, token_count, after=(), block=512):
    features = rows[0].shape[1]
    table_spec = pl.BlockSpec(slots.shape, lambda i: (0, 0))
    out = jax.ShapeDtypeStruct((token_count, features), jnp.bfloat16)
    return pl.pallas_call(
        merge_body,
        name="merge_rows",
        grid=(features // block,),
        out_shape=(out,) * SIDE,
        in_specs=[table_spec] * 2
        + [pl.BlockSpec((SIDE * CAP, block), lambda i: (0, i))] * TARGETS
        + [UNTOUCHED] * len(after),
        out_specs=(pl.BlockSpec((token_count, block), lambda i: (0, i)),) * SIDE,
        compiler_params=pltpu.CompilerParams(vmem_limit_bytes=32 * MIB),
    )(slots, gates, *rows, *after)


def expert_body(hidden_steps, gate_ref, up_ref, down_ref, *refs):
    row_refs = refs[:TARGETS]
    out_refs = refs[-TARGETS - 2 : -2]
    rows_scratch, hidden_scratch = refs[-2:]
    step = pl.program_id(0)
    count = SIDE * CAP
    block = gate_ref.shape[1]

    @pl.when(step == 0)
    def _():
        rows_scratch[...] = jnp.concatenate(
            [ref[...].astype(jnp.float32) for ref in row_refs], axis=0
        ).astype(jnp.bfloat16)

    @pl.when(step < hidden_steps)
    def _():
        rows = rows_scratch[...]
        gate_act = jnp.dot(rows, gate_ref[...], preferred_element_type=jnp.float32)
        up_act = jnp.dot(rows, up_ref[...], preferred_element_type=jnp.float32)
        hidden_scratch[:, pl.ds(pl.multiple_of(step * block, block), block)] = (
            jax.nn.silu(gate_act) * up_act
        ).astype(jnp.bfloat16)

    @pl.when(step >= hidden_steps)
    def _():
        finished = jnp.dot(hidden_scratch[...], down_ref[...], preferred_element_type=jnp.float32)
        for e, ref in enumerate(out_refs):
            ref[...] = finished[e * count : (e + 1) * count].astype(jnp.bfloat16)


def expert_rows(rows, weights, after=(), block=256, out_block=512):
    gate_mat, up_mat, down_mat = weights
    features, hidden_count = gate_mat.shape
    count = SIDE * CAP
    hidden_steps = hidden_count // block
    out = jax.ShapeDtypeStruct((count, features), jnp.bfloat16)
    hidden_spec = pl.BlockSpec((features, block), lambda i: (0, jnp.minimum(i, hidden_steps - 1)))
    return pl.pallas_call(
        partial(expert_body, hidden_steps),
        name="expert_rows",
        grid=(hidden_steps + features // out_block,),
        out_shape=(out,) * TARGETS,
        in_specs=[
            hidden_spec,
            hidden_spec,
            pl.BlockSpec(
                (hidden_count, out_block), lambda i: (0, jnp.maximum(i - hidden_steps, 0))
            ),
        ]
        + [pl.BlockSpec((count, features), lambda i: (0, 0))] * TARGETS
        + [UNTOUCHED] * len(after),
        out_specs=(
            pl.BlockSpec((count, out_block), lambda i: (0, jnp.maximum(i - hidden_steps, 0))),
        )
        * TARGETS,
        scratch_shapes=[
            pltpu.VMEM((TARGETS * count, features), jnp.bfloat16),
            pltpu.VMEM((TARGETS * count, hidden_count), jnp.bfloat16),
        ],
        compiler_params=pltpu.CompilerParams(vmem_limit_bytes=40 * MIB),
    )(gate_mat, up_mat, down_mat, *rows, *after)


def grad_body(tangents_ref, *refs):
    row_refs, out_ref = (refs[:-1], refs[-1])
    rows = jnp.concatenate([ref[...] for ref in row_refs], axis=0)
    grad = jnp.dot(tangents_ref[...], rows, preferred_element_type=jnp.float32)
    own_rows = out_ref.shape[2]
    for e in range(out_ref.shape[0]):
        out_ref[e] = grad[:, e * own_rows : (e + 1) * own_rows].astype(jnp.bfloat16)


def summed_grad(normed_rows, tangents):
    expert_count = lax.axis_size("expert")
    own_rows = normed_rows[0].shape[1] // expert_count
    partial_grad = pl.pallas_call(
        grad_body,
        name="key_grad",
        out_shape=jax.ShapeDtypeStruct((expert_count, tangents.shape[0], own_rows), jnp.bfloat16),
        compiler_params=pltpu.CompilerParams(vmem_limit_bytes=32 * MIB),
    )(tangents, *normed_rows)
    gathered = lax.all_to_all(partial_grad, "expert", split_axis=0, concat_axis=0, tiled=True)
    return jnp.sum(gathered.astype(jnp.float32), axis=0).T


def on_device(
    down_tokens,
    up_tokens,
    norm_gain,
    w_gate,
    w_up,
    w_down,
    down_ids,
    down_gates,
    up_ids,
    up_gates,
    key_cotangent,
):
    segment_count = lax.axis_size("pipe")
    segment_pos = lax.axis_index("pipe")
    micro_count = down_tokens.shape[0]
    norm_scale = norm_gain[0]
    weights = (w_gate[0, 0], w_up[0, 0], w_down[0, 0])
    down_first = segment_pos < segment_count // 2
    first_step = jnp.minimum(segment_pos, segment_count - 1 - segment_pos)
    half = segment_count // 2
    carried = [
        jnp.where(segment_pos == 0, down_tokens[micro], up_tokens[micro])
        for micro in range(micro_count)
    ]
    route_ids = jnp.concatenate(
        [jnp.where(down_first, down_ids[0], up_ids[0]), jnp.where(down_first, up_ids[0], down_ids[0])]
    )
    route_gates = jnp.concatenate(
        [
            jnp.where(down_first, down_gates[0], up_gates[0]),
            jnp.where(down_first, up_gates[0], down_gates[0]),
        ]
    )
    normed = normalize(carried[0], norm_scale)
    route_ids, route_gates, normed = lax.optimization_barrier((route_ids, route_gates, normed))
    slots, gates = routing_tables(route_ids, route_gates)
    turn_order = [(step, micro) for step in range(segment_count) for micro in range(micro_count)]
    outputs = {}
    normed_rows = {}
    returned = {}
    expert_done = ()
    pending = None

    def finish(step, micro, after):
        table = step // half * micro_count + micro
        token_count = carried[micro].shape[0]
        sums = merge_rows(
            slots[table], gates[table], returned[step, micro], token_count, after
        )
        total = carried[micro].astype(jnp.float32)
        for own_sum in along_first(sums, back=True):
            total = total + own_sum.astype(jnp.float32)
        output = total.astype(jnp.bfloat16)
        outputs[step, micro] = output
        if step + 1 < segment_count:
            carried[micro] = lax.ppermute(
                output,
                "pipe",
                [(step, step + 1), (segment_count - 1 - step, segment_count - 2 - step)],
            )
        return (sums[0],)

    for turn_index, (step, micro) in enumerate(turn_order):
        if turn_index:
            normed = normalize(carried[micro], norm_scale)
        normed_rows[step, micro] = normed
        table = step // half * micro_count + micro
        picked = pick_rows(
            slots[table],
            along_first([normed] * SIDE),
            expert_done if turn_index >= 2 else (),
        )
        arrived = along_second(picked)
        merged = finish(*pending, (picked[0],)) if pending else ()
        finished = expert_rows(arrived, weights, merged)
        expert_done = (finished[0],)
        returned[step, micro] = along_second(finished, back=True)
        pending = (step, micro)
    finish(*pending, ())

    def turns(values):
        chosen = []
        for turn in range(2):
            for micro in range(micro_count):
                value = values[turn * half, micro]
                for offset in range(1, half):
                    step = turn * half + offset
                    here = (first_step if turn == 0 else segment_count - 1 - first_step) == step
                    value = jnp.where(here, values[step, micro], value)
                chosen.append(value)
        return chosen

    turn_outputs = turns(outputs)
    first, second = (jnp.stack(turn_outputs[:micro_count]), jnp.stack(turn_outputs[micro_count:]))
    down_states = jnp.where(down_first, first, second)
    up_states = jnp.where(down_first, second, first)
    def tangents_of(step, micro):
        turn = step // half
        here = (first_step if turn == 0 else segment_count - 1 - first_step) == step
        first_turn = down_first if turn == 0 else ~down_first
        value = jnp.where(first_turn, key_cotangent[0, 0, micro], key_cotangent[0, 1, micro])
        return jnp.where(here, value, jnp.zeros_like(value))

    tangents = jnp.concatenate([tangents_of(*key) for key in turn_order]).T
    key_grad = summed_grad([normed_rows[key] for key in turn_order], tangents)
    return (down_states[None], up_states[None], key_grad[None])


def solution(mesh):
    return jax.shard_map(
        on_device,
        mesh=mesh,
        in_specs=(
            P(None, "expert", None),
            P(None, "expert", None),
            P("pipe", None),
            P("pipe", "expert", None, None),
            P("pipe", "expert", None, None),
            P("pipe", "expert", None, None),
            P("pipe", None, "expert", None),
            P("pipe", None, "expert", None),
            P("pipe", None, "expert", None),
            P("pipe", None, "expert", None),
            P("pipe", None, None, "expert", None),
        ),
        out_specs=(
            P("pipe", None, "expert", None),
            P("pipe", None, "expert", None),
            P("pipe", "expert", None),
        ),
        check_vma=False,
    )
```

```python
from functools import partial

import jax
import jax.numpy as jnp
from jax import lax
from jax.experimental import pallas as pl
from jax.experimental.pallas import tpu as pltpu
from jax.sharding import PartitionSpec as P

EPSILON = 1e-06
UNTOUCHED = pl.BlockSpec(memory_space=pl.ANY)
SIDE = 4
CAP = 10
TARGETS = 2 * SIDE
MIB = 1 << 20


def device_at(x, y, core):
    return (x % SIDE) * 2 * SIDE + (y % SIDE) * 2 + core


def first_line(shift):
    pairs = []
    for x in range(SIDE):
        for y in range(SIDE):
            pairs.append((device_at(x, y, 0), device_at(x + shift, y, 0)))
            pairs.append((device_at(x, y, 1), device_at(x, y + shift, 1)))
    return pairs


def second_line(shift, flip):
    pairs = []
    for x in range(SIDE):
        for y in range(SIDE):
            pairs.append((device_at(x, y, 0), device_at(x, y + shift, flip)))
            pairs.append((device_at(x, y, 1), device_at(x + shift, y, 1 - flip)))
    return pairs


def backwards(pairs):
    return [(target, source) for source, target in pairs]


HOPS = [(shift, flip) for shift in range(SIDE) for flip in range(2)]


def along_first(blocks, back=False):
    moved = []
    for shift, block in enumerate(blocks):
        pairs = first_line(shift)
        moved.append(
            lax.ppermute(block, "expert", backwards(pairs) if back else pairs) if shift else block
        )
    return moved


def along_second(blocks, back=False):
    moved = []
    for (shift, flip), block in zip(HOPS, blocks):
        pairs = second_line(shift, flip)
        stays = shift == 0 and flip == 0
        moved.append(
            block if stays else lax.ppermute(block, "expert", backwards(pairs) if back else pairs)
        )
    return moved


def normalize(carried, norm_scale):
    values = carried.astype(jnp.float32)
    inv_rms = lax.rsqrt(jnp.mean(values * values, axis=-1, keepdims=True) + EPSILON)
    return (values * inv_rms * norm_scale).astype(jnp.bfloat16)


def routing_tables(route_ids, route_gates):
    block_count, token_count, pick_count = route_ids.shape
    packed = jnp.concatenate(
        [jnp.swapaxes(route_ids, 1, 2).astype(jnp.float32), jnp.swapaxes(route_gates, 1, 2)], axis=1
    )
    gathered = jnp.concatenate(along_first([packed] * SIDE), axis=-1)
    ids, gates = (gathered[:, :pick_count], gathered[:, pick_count:])
    position = lax.axis_index("expert")
    x, y, core = (position // (2 * SIDE), (position // 2) % SIDE, position % 2)
    shift = jnp.arange(TARGETS, dtype=jnp.int32) // 2
    flip = jnp.arange(TARGETS, dtype=jnp.int32) % 2
    experts = jnp.where(
        core == 0,
        x * 2 * SIDE + ((y + shift) % SIDE) * 2 + flip,
        ((x + shift) % SIDE) * 2 * SIDE + y * 2 + 1 - flip,
    ).astype(jnp.float32)
    matches = (ids[:, None] == experts[None, :, None, None]).astype(jnp.float32)
    chosen = jnp.sum(matches, axis=2)
    gate_of = jnp.sum(matches * gates[:, None], axis=2)
    lane = jnp.arange(SIDE * token_count, dtype=jnp.int32)
    earlier = (lane[:, None] // token_count == lane[None, :] // token_count) & (
        lane[:, None] < lane[None, :]
    )
    rank = jnp.einsum(
        "bet,tu->beu",
        chosen.astype(jnp.bfloat16),
        earlier.astype(jnp.bfloat16),
        preferred_element_type=jnp.float32,
    )
    return jnp.where(chosen > 0, rank, -1.0), gate_of


def slot_pattern(line_count, token_count):
    rows, columns = (line_count * CAP, line_count * token_count)
    row = lax.broadcasted_iota(jnp.int32, (rows, columns), 0)
    column = lax.broadcasted_iota(jnp.int32, (rows, columns), 1)
    return jnp.where(row // CAP == column // token_count, row % CAP, -2).astype(jnp.float32)


def pick_body(slots_ref, *refs):
    row_refs, out_refs = (refs[:SIDE], refs[-TARGETS:])
    token_count = row_refs[0].shape[0]
    pattern = slot_pattern(SIDE, token_count)
    table = jnp.concatenate(
        [(slots_ref[e : e + 1, :] == pattern).astype(jnp.float32) for e in range(TARGETS)], axis=0
    ).astype(jnp.bfloat16)
    rows = jnp.concatenate([ref[...] for ref in row_refs], axis=0)
    picked = jnp.dot(table, rows, preferred_element_type=jnp.float32)
    count = SIDE * CAP
    for e, ref in enumerate(out_refs):
        ref[...] = picked[e * count : (e + 1) * count].astype(jnp.bfloat16)


def pick_rows(slots, rows, after=(), block=512):
    token_count, features = rows[0].shape
    table_spec = pl.BlockSpec(slots.shape, lambda i: (0, 0))
    out = jax.ShapeDtypeStruct((SIDE * CAP, features), jnp.bfloat16)
    return pl.pallas_call(
        pick_body,
        name="pick_rows",
        grid=(features // block,),
        out_shape=(out,) * TARGETS,
        in_specs=[table_spec]
        + [pl.BlockSpec((token_count, block), lambda i: (0, i))] * SIDE
        + [UNTOUCHED] * len(after),
        out_specs=(pl.BlockSpec((SIDE * CAP, block), lambda i: (0, i)),) * TARGETS,
        compiler_params=pltpu.CompilerParams(vmem_limit_bytes=32 * MIB),
    )(slots, *rows, *after)


def merge_body(slots_ref, gates_ref, *refs):
    row_refs, out_refs = (refs[:TARGETS], refs[-SIDE:])
    token_count = out_refs[0].shape[0]
    pattern = slot_pattern(SIDE, token_count)
    weights = jnp.concatenate(
        [
            jnp.where(slots_ref[e : e + 1, :] == pattern, gates_ref[e : e + 1, :], 0.0)
            for e in range(TARGETS)
        ],
        axis=0,
    )
    rows = jnp.concatenate([ref[...].astype(jnp.float32) for ref in row_refs], axis=0)
    merged = jnp.dot(
        weights.T.astype(jnp.bfloat16),
        rows.astype(jnp.bfloat16),
        preferred_element_type=jnp.float32,
    )
    for m, ref in enumerate(out_refs):
        ref[...] = merged[m * token_count : (m + 1) * token_count].astype(jnp.bfloat16)


def merge_rows(slots, gates, rows, token_count, after=(), block=512):
    features = rows[0].shape[1]
    table_spec = pl.BlockSpec(slots.shape, lambda i: (0, 0))
    out = jax.ShapeDtypeStruct((token_count, features), jnp.bfloat16)
    return pl.pallas_call(
        merge_body,
        name="merge_rows",
        grid=(features // block,),
        out_shape=(out,) * SIDE,
        in_specs=[table_spec] * 2
        + [pl.BlockSpec((SIDE * CAP, block), lambda i: (0, i))] * TARGETS
        + [UNTOUCHED] * len(after),
        out_specs=(pl.BlockSpec((token_count, block), lambda i: (0, i)),) * SIDE,
        compiler_params=pltpu.CompilerParams(vmem_limit_bytes=32 * MIB),
    )(slots, gates, *rows, *after)


def expert_body(gate_ref, up_ref, down_ref, *refs):
    row_refs, out_refs = (refs[:TARGETS], refs[-TARGETS - 2 : -2])
    rows_scratch, sum_scratch = refs[-2:]
    step = pl.program_id(0)
    count = SIDE * CAP

    @pl.when(step == 0)
    def _():
        rows_scratch[...] = jnp.concatenate(
            [ref[...].astype(jnp.float32) for ref in row_refs], axis=0
        ).astype(jnp.bfloat16)

    rows = rows_scratch[...]
    gate_act = jnp.dot(rows, gate_ref[...], preferred_element_type=jnp.float32)
    up_act = jnp.dot(rows, up_ref[...], preferred_element_type=jnp.float32)
    hidden = (jax.nn.silu(gate_act) * up_act).astype(jnp.bfloat16)
    part = jnp.dot(hidden, down_ref[...], preferred_element_type=jnp.float32)

    @pl.when(step == 0)
    def _():
        sum_scratch[...] = part

    @pl.when(step > 0)
    def _():
        sum_scratch[...] += part

    @pl.when(step == pl.num_programs(0) - 1)
    def _():
        for e, ref in enumerate(out_refs):
            ref[...] = sum_scratch[e * count : (e + 1) * count, :].astype(jnp.bfloat16)


def expert_rows(rows, weights, after=(), block=256):
    gate_mat, up_mat, down_mat = weights
    features, hidden_count = gate_mat.shape
    count = SIDE * CAP
    row_spec = pl.BlockSpec((count, features), lambda i: (0, 0))
    out = jax.ShapeDtypeStruct((count, features), jnp.bfloat16)
    return pl.pallas_call(
        expert_body,
        name="expert_rows",
        grid=(hidden_count // block,),
        out_shape=(out,) * TARGETS,
        in_specs=[
            pl.BlockSpec((features, block), lambda i: (0, i)),
            pl.BlockSpec((features, block), lambda i: (0, i)),
            pl.BlockSpec((block, features), lambda i: (i, 0)),
        ]
        + [row_spec] * TARGETS
        + [UNTOUCHED] * len(after),
        out_specs=(row_spec,) * TARGETS,
        scratch_shapes=[
            pltpu.VMEM((TARGETS * count, features), jnp.bfloat16),
            pltpu.VMEM((TARGETS * count, features), jnp.float32),
        ],
        compiler_params=pltpu.CompilerParams(vmem_limit_bytes=50 * MIB),
    )(gate_mat, up_mat, down_mat, *rows, *after)


def grad_body(tangents_ref, *refs):
    row_refs, out_ref = (refs[:-1], refs[-1])
    rows = jnp.concatenate([ref[...] for ref in row_refs], axis=0)
    grad = jnp.dot(tangents_ref[...], rows, preferred_element_type=jnp.float32)
    own_rows = out_ref.shape[2]
    for e in range(out_ref.shape[0]):
        out_ref[e] = grad[:, e * own_rows : (e + 1) * own_rows].astype(jnp.bfloat16)


def summed_grad(normed_rows, tangents):
    expert_count = lax.axis_size("expert")
    own_rows = normed_rows[0].shape[1] // expert_count
    partial_grad = pl.pallas_call(
        grad_body,
        name="key_grad",
        out_shape=jax.ShapeDtypeStruct((expert_count, tangents.shape[0], own_rows), jnp.bfloat16),
        compiler_params=pltpu.CompilerParams(vmem_limit_bytes=32 * MIB),
    )(tangents, *normed_rows)
    gathered = lax.all_to_all(partial_grad, "expert", split_axis=0, concat_axis=0, tiled=True)
    return jnp.sum(gathered.astype(jnp.float32), axis=0).T


def on_device(
    down_tokens,
    up_tokens,
    norm_gain,
    w_gate,
    w_up,
    w_down,
    down_ids,
    down_gates,
    up_ids,
    up_gates,
    key_cotangent,
):
    segment_count = lax.axis_size("pipe")
    segment_pos = lax.axis_index("pipe")
    micro_count = down_tokens.shape[0]
    norm_scale = norm_gain[0]
    weights = (w_gate[0, 0], w_up[0, 0], w_down[0, 0])
    down_first = segment_pos < segment_count // 2
    first_step = jnp.minimum(segment_pos, segment_count - 1 - segment_pos)
    half = segment_count // 2
    carried = [
        jnp.where(segment_pos == 0, down_tokens[micro], up_tokens[micro])
        for micro in range(micro_count)
    ]
    route_ids = jnp.concatenate(
        [jnp.where(down_first, down_ids[0], up_ids[0]), jnp.where(down_first, up_ids[0], down_ids[0])]
    )
    route_gates = jnp.concatenate(
        [
            jnp.where(down_first, down_gates[0], up_gates[0]),
            jnp.where(down_first, up_gates[0], down_gates[0]),
        ]
    )
    normed = normalize(carried[0], norm_scale)
    route_ids, route_gates, normed = lax.optimization_barrier((route_ids, route_gates, normed))
    slots, gates = routing_tables(route_ids, route_gates)
    turn_order = [(step, micro) for step in range(segment_count) for micro in range(micro_count)]
    outputs = {}
    normed_rows = {}
    for step in range(segment_count):
        picked = {}
        for micro in range(micro_count):
            if (step, micro) != (0, 0):
                normed = normalize(carried[micro], norm_scale)
            normed_rows[step, micro] = normed
            table = step // half * micro_count + micro
            before = (picked[micro - 1][0],) if micro else ()
            picked[micro] = pick_rows(slots[table], along_first([normed] * SIDE), before)
        finished = {}
        before = (picked[micro_count - 1][0],)
        for micro in range(micro_count):
            finished[micro] = expert_rows(along_second(picked[micro]), weights, before)
            before = (finished[micro][0],)
        for micro in range(micro_count):
            table = step // half * micro_count + micro
            returned = along_second(finished[micro], back=True)
            sums = merge_rows(
                slots[table], gates[table], returned, carried[micro].shape[0], before
            )
            before = (sums[0],)
            total = carried[micro].astype(jnp.float32)
            for own_sum in along_first(sums, back=True):
                total = total + own_sum.astype(jnp.float32)
            outputs[step, micro] = total.astype(jnp.bfloat16)
            if step + 1 < segment_count:
                carried[micro] = lax.ppermute(
                    outputs[step, micro],
                    "pipe",
                    [(step, step + 1), (segment_count - 1 - step, segment_count - 2 - step)],
                )

    def turns(values):
        chosen = []
        for turn in range(2):
            for micro in range(micro_count):
                value = values[turn * half, micro]
                for offset in range(1, half):
                    step = turn * half + offset
                    here = (first_step if turn == 0 else segment_count - 1 - first_step) == step
                    value = jnp.where(here, values[step, micro], value)
                chosen.append(value)
        return chosen

    turn_outputs = turns(outputs)
    first, second = (jnp.stack(turn_outputs[:micro_count]), jnp.stack(turn_outputs[micro_count:]))
    down_states = jnp.where(down_first, first, second)
    up_states = jnp.where(down_first, second, first)
    def tangents_of(step, micro):
        turn = step // half
        here = (first_step if turn == 0 else segment_count - 1 - first_step) == step
        first_turn = down_first if turn == 0 else ~down_first
        value = jnp.where(first_turn, key_cotangent[0, 0, micro], key_cotangent[0, 1, micro])
        return jnp.where(here, value, jnp.zeros_like(value))

    tangents = jnp.concatenate([tangents_of(*key) for key in turn_order]).T
    key_grad = summed_grad([normed_rows[key] for key in turn_order], tangents)
    return (down_states[None], up_states[None], key_grad[None])


def solution(mesh):
    return jax.shard_map(
        on_device,
        mesh=mesh,
        in_specs=(
            P(None, "expert", None),
            P(None, "expert", None),
            P("pipe", None),
            P("pipe", "expert", None, None),
            P("pipe", "expert", None, None),
            P("pipe", "expert", None, None),
            P("pipe", None, "expert", None),
            P("pipe", None, "expert", None),
            P("pipe", None, "expert", None),
            P("pipe", None, "expert", None),
            P("pipe", None, None, "expert", None),
        ),
        out_specs=(
            P("pipe", None, "expert", None),
            P("pipe", None, "expert", None),
            P("pipe", "expert", None),
        ),
        check_vma=False,
    )
```

```python
from functools import partial

import jax
import jax.numpy as jnp
from jax import lax
from jax.experimental import pallas as pl
from jax.experimental.pallas import tpu as pltpu
from jax.sharding import PartitionSpec as P

EPSILON = 1e-06
UNTOUCHED = pl.BlockSpec(memory_space=pl.ANY)
SIDE = 4
CAP = 10
TARGETS = 2 * SIDE
MIB = 1 << 20


def device_at(x, y, core):
    return (x % SIDE) * 2 * SIDE + (y % SIDE) * 2 + core


def first_line(shift):
    pairs = []
    for x in range(SIDE):
        for y in range(SIDE):
            pairs.append((device_at(x, y, 0), device_at(x + shift, y, 0)))
            pairs.append((device_at(x, y, 1), device_at(x, y + shift, 1)))
    return pairs


def second_line(shift, flip):
    pairs = []
    for x in range(SIDE):
        for y in range(SIDE):
            pairs.append((device_at(x, y, 0), device_at(x, y + shift, flip)))
            pairs.append((device_at(x, y, 1), device_at(x + shift, y, 1 - flip)))
    return pairs


def backwards(pairs):
    return [(target, source) for source, target in pairs]


HOPS = [(shift, flip) for shift in range(SIDE) for flip in range(2)]


def along_first(blocks, back=False):
    moved = []
    for shift, block in enumerate(blocks):
        pairs = first_line(shift)
        moved.append(
            lax.ppermute(block, "expert", backwards(pairs) if back else pairs) if shift else block
        )
    return moved


def along_second(blocks, back=False):
    moved = []
    for (shift, flip), block in zip(HOPS, blocks):
        pairs = second_line(shift, flip)
        stays = shift == 0 and flip == 0
        moved.append(
            block if stays else lax.ppermute(block, "expert", backwards(pairs) if back else pairs)
        )
    return moved


def normalize_body(carried_ref, scale_ref, out_ref):
    values = carried_ref[...].astype(jnp.float32)
    inv_rms = lax.rsqrt(jnp.mean(values * values, axis=-1, keepdims=True) + EPSILON)
    out_ref[...] = (values * inv_rms * scale_ref[...]).astype(jnp.bfloat16)


def normalize(carried, norm_scale):
    return pl.pallas_call(
        normalize_body,
        name="normalize",
        out_shape=jax.ShapeDtypeStruct(carried.shape, jnp.bfloat16),
        compiler_params=pltpu.CompilerParams(vmem_limit_bytes=8 * MIB),
    )(carried, norm_scale)


def routing_tables(route_ids, route_gates):
    block_count, token_count, pick_count = route_ids.shape
    packed = jnp.concatenate(
        [jnp.swapaxes(route_ids, 1, 2).astype(jnp.float32), jnp.swapaxes(route_gates, 1, 2)], axis=1
    )
    gathered = jnp.concatenate(along_first([packed] * SIDE), axis=-1)
    ids, gates = (gathered[:, :pick_count], gathered[:, pick_count:])
    position = lax.axis_index("expert")
    x, y, core = (position // (2 * SIDE), (position // 2) % SIDE, position % 2)
    shift = jnp.arange(TARGETS, dtype=jnp.int32) // 2
    flip = jnp.arange(TARGETS, dtype=jnp.int32) % 2
    experts = jnp.where(
        core == 0,
        x * 2 * SIDE + ((y + shift) % SIDE) * 2 + flip,
        ((x + shift) % SIDE) * 2 * SIDE + y * 2 + 1 - flip,
    ).astype(jnp.float32)
    matches = (ids[:, None] == experts[None, :, None, None]).astype(jnp.float32)
    chosen = jnp.sum(matches, axis=2)
    gate_of = jnp.sum(matches * gates[:, None], axis=2)
    lane = jnp.arange(SIDE * token_count, dtype=jnp.int32)
    earlier = (lane[:, None] // token_count == lane[None, :] // token_count) & (
        lane[:, None] < lane[None, :]
    )
    rank = jnp.einsum(
        "bet,tu->beu",
        chosen.astype(jnp.bfloat16),
        earlier.astype(jnp.bfloat16),
        preferred_element_type=jnp.float32,
    )
    return jnp.where(chosen > 0, rank, -1.0), gate_of


def slot_pattern(line_count, token_count):
    rows, columns = (line_count * CAP, line_count * token_count)
    row = lax.broadcasted_iota(jnp.int32, (rows, columns), 0)
    column = lax.broadcasted_iota(jnp.int32, (rows, columns), 1)
    return jnp.where(row // CAP == column // token_count, row % CAP, -2).astype(jnp.float32)


def pick_body(slots_ref, *refs):
    row_refs, out_refs = (refs[:SIDE], refs[-TARGETS:])
    token_count = row_refs[0].shape[0]
    pattern = slot_pattern(SIDE, token_count)
    table = jnp.concatenate(
        [(slots_ref[e : e + 1, :] == pattern).astype(jnp.float32) for e in range(TARGETS)], axis=0
    ).astype(jnp.bfloat16)
    rows = jnp.concatenate([ref[...] for ref in row_refs], axis=0)
    picked = jnp.dot(table, rows, preferred_element_type=jnp.float32)
    count = SIDE * CAP
    for e, ref in enumerate(out_refs):
        ref[...] = picked[e * count : (e + 1) * count].astype(jnp.bfloat16)


def pick_rows(slots, rows, after=()):
    token_count, features = rows[0].shape
    block = features
    table_spec = pl.BlockSpec(slots.shape, lambda i: (0, 0))
    out = jax.ShapeDtypeStruct((SIDE * CAP, features), jnp.bfloat16)
    return pl.pallas_call(
        pick_body,
        name="pick_rows",
        grid=(features // block,),
        out_shape=(out,) * TARGETS,
        in_specs=[table_spec]
        + [pl.BlockSpec((token_count, block), lambda i: (0, i))] * SIDE
        + [UNTOUCHED] * len(after),
        out_specs=(pl.BlockSpec((SIDE * CAP, block), lambda i: (0, i)),) * TARGETS,
        compiler_params=pltpu.CompilerParams(vmem_limit_bytes=32 * MIB),
    )(slots, *rows, *after)


def merge_body(slots_ref, gates_ref, *refs):
    row_refs, out_refs = (refs[:TARGETS], refs[-SIDE:])
    token_count = out_refs[0].shape[0]
    pattern = slot_pattern(SIDE, token_count)
    weights = jnp.concatenate(
        [
            jnp.where(slots_ref[e : e + 1, :] == pattern, gates_ref[e : e + 1, :], 0.0)
            for e in range(TARGETS)
        ],
        axis=0,
    )
    rows = jnp.concatenate([ref[...].astype(jnp.float32) for ref in row_refs], axis=0)
    merged = jnp.dot(
        weights.T.astype(jnp.bfloat16),
        rows.astype(jnp.bfloat16),
        preferred_element_type=jnp.float32,
    )
    for m, ref in enumerate(out_refs):
        ref[...] = merged[m * token_count : (m + 1) * token_count].astype(jnp.bfloat16)


def merge_rows(slots, gates, rows, token_count, after=()):
    features = rows[0].shape[1]
    block = features
    table_spec = pl.BlockSpec(slots.shape, lambda i: (0, 0))
    out = jax.ShapeDtypeStruct((token_count, features), jnp.bfloat16)
    return pl.pallas_call(
        merge_body,
        name="merge_rows",
        grid=(features // block,),
        out_shape=(out,) * SIDE,
        in_specs=[table_spec] * 2
        + [pl.BlockSpec((SIDE * CAP, block), lambda i: (0, i))] * TARGETS
        + [UNTOUCHED] * len(after),
        out_specs=(pl.BlockSpec((token_count, block), lambda i: (0, i)),) * SIDE,
        compiler_params=pltpu.CompilerParams(vmem_limit_bytes=32 * MIB),
    )(slots, gates, *rows, *after)


def expert_body(gate_ref, up_ref, down_ref, *refs):
    row_refs, out_refs = (refs[:TARGETS], refs[-TARGETS - 2 : -2])
    rows_scratch, sum_scratch = refs[-2:]
    step = pl.program_id(0)
    count = SIDE * CAP

    @pl.when(step == 0)
    def _():
        rows_scratch[...] = jnp.concatenate(
            [ref[...].astype(jnp.float32) for ref in row_refs], axis=0
        ).astype(jnp.bfloat16)

    rows = rows_scratch[...]
    gate_act = jnp.dot(rows, gate_ref[...], preferred_element_type=jnp.float32)
    up_act = jnp.dot(rows, up_ref[...], preferred_element_type=jnp.float32)
    hidden = (jax.nn.silu(gate_act) * up_act).astype(jnp.bfloat16)
    part = jnp.dot(hidden, down_ref[...], preferred_element_type=jnp.float32)

    @pl.when(step == 0)
    def _():
        sum_scratch[...] = part

    @pl.when(step > 0)
    def _():
        sum_scratch[...] += part

    @pl.when(step == pl.num_programs(0) - 1)
    def _():
        for e, ref in enumerate(out_refs):
            ref[...] = sum_scratch[e * count : (e + 1) * count, :].astype(jnp.bfloat16)


def expert_rows(rows, weights, after=(), block=256):
    gate_mat, up_mat, down_mat = weights
    features, hidden_count = gate_mat.shape
    count = SIDE * CAP
    row_spec = pl.BlockSpec((count, features), lambda i: (0, 0))
    out = jax.ShapeDtypeStruct((count, features), jnp.bfloat16)
    return pl.pallas_call(
        expert_body,
        name="expert_rows",
        grid=(hidden_count // block,),
        out_shape=(out,) * TARGETS,
        in_specs=[
            pl.BlockSpec((features, block), lambda i: (0, i)),
            pl.BlockSpec((features, block), lambda i: (0, i)),
            pl.BlockSpec((block, features), lambda i: (i, 0)),
        ]
        + [row_spec] * TARGETS
        + [UNTOUCHED] * len(after),
        out_specs=(row_spec,) * TARGETS,
        scratch_shapes=[
            pltpu.VMEM((TARGETS * count, features), jnp.bfloat16),
            pltpu.VMEM((TARGETS * count, features), jnp.float32),
        ],
        compiler_params=pltpu.CompilerParams(vmem_limit_bytes=50 * MIB),
    )(gate_mat, up_mat, down_mat, *rows, *after)


def grad_body(tangents_ref, *refs):
    row_refs, out_ref = (refs[:-1], refs[-1])
    rows = jnp.concatenate([ref[...] for ref in row_refs], axis=0)
    grad = jnp.dot(tangents_ref[...], rows, preferred_element_type=jnp.float32)
    own_rows = out_ref.shape[2]
    for e in range(out_ref.shape[0]):
        out_ref[e] = grad[:, e * own_rows : (e + 1) * own_rows].astype(jnp.bfloat16)


def summed_grad(normed_rows, tangents):
    expert_count = lax.axis_size("expert")
    own_rows = normed_rows[0].shape[1] // expert_count
    partial_grad = pl.pallas_call(
        grad_body,
        name="key_grad",
        out_shape=jax.ShapeDtypeStruct((expert_count, tangents.shape[0], own_rows), jnp.bfloat16),
        compiler_params=pltpu.CompilerParams(vmem_limit_bytes=32 * MIB),
    )(tangents, *normed_rows)
    gathered = lax.all_to_all(partial_grad, "expert", split_axis=0, concat_axis=0, tiled=True)
    return jnp.sum(gathered.astype(jnp.float32), axis=0).T


def placed_body(segment_count, flags_ref, *refs):
    state_refs, down_ref, up_ref = (refs[:-2], refs[-2], refs[-1])
    micro_count = down_ref.shape[0]
    outer, down_first = (flags_ref[0] == 1, flags_ref[1] == 1)
    last = segment_count - 1
    for micro in range(micro_count):
        first = jnp.where(
            outer, state_refs[micro][...], state_refs[micro_count + micro][...]
        )
        second = jnp.where(
            outer,
            state_refs[last * micro_count + micro][...],
            state_refs[(last - 1) * micro_count + micro][...],
        )
        down_ref[micro] = jnp.where(down_first, first, second)
        up_ref[micro] = jnp.where(down_first, second, first)


def placed_states(flags, states, segment_count, micro_count):
    assert segment_count == 4
    out = jax.ShapeDtypeStruct((micro_count,) + states[0].shape, states[0].dtype)
    return pl.pallas_call(
        partial(placed_body, segment_count),
        name="placed_states",
        out_shape=(out, out),
        in_specs=[pl.BlockSpec(memory_space=pltpu.SMEM)]
        + [pl.BlockSpec(memory_space=pltpu.VMEM)] * len(states),
        compiler_params=pltpu.CompilerParams(vmem_limit_bytes=16 * MIB),
    )(flags, *states)


def on_device(
    down_tokens,
    up_tokens,
    norm_gain,
    w_gate,
    w_up,
    w_down,
    down_ids,
    down_gates,
    up_ids,
    up_gates,
    key_cotangent,
):
    segment_count = lax.axis_size("pipe")
    segment_pos = lax.axis_index("pipe")
    micro_count = down_tokens.shape[0]
    norm_scale = norm_gain
    weights = (w_gate[0, 0], w_up[0, 0], w_down[0, 0])
    down_first = segment_pos < segment_count // 2
    first_step = jnp.minimum(segment_pos, segment_count - 1 - segment_pos)
    half = segment_count // 2
    carried = [
        jnp.where(segment_pos == 0, down_tokens[micro], up_tokens[micro])
        for micro in range(micro_count)
    ]
    route_ids = jnp.concatenate(
        [jnp.where(down_first, down_ids[0], up_ids[0]), jnp.where(down_first, up_ids[0], down_ids[0])]
    )
    route_gates = jnp.concatenate(
        [
            jnp.where(down_first, down_gates[0], up_gates[0]),
            jnp.where(down_first, up_gates[0], down_gates[0]),
        ]
    )
    normed = normalize(carried[0], norm_scale)
    route_ids, route_gates, normed = lax.optimization_barrier((route_ids, route_gates, normed))
    slots, gates = routing_tables(route_ids, route_gates)
    turn_order = [(step, micro) for step in range(segment_count) for micro in range(micro_count)]
    outputs = {}
    normed_rows = {}
    for step in range(segment_count):
        picked = {}
        for micro in range(micro_count):
            if (step, micro) != (0, 0):
                normed = normalize(carried[micro], norm_scale)
            normed_rows[step, micro] = normed
            table = step // half * micro_count + micro
            before = (picked[micro - 1][0],) if micro else ()
            picked[micro] = pick_rows(slots[table], along_first([normed] * SIDE), before)
        finished = {}
        before = (picked[micro_count - 1][0],)
        for micro in range(micro_count):
            finished[micro] = expert_rows(along_second(picked[micro]), weights, before)
            before = (finished[micro][0],)
        for micro in range(micro_count):
            table = step // half * micro_count + micro
            returned = along_second(finished[micro], back=True)
            sums = merge_rows(
                slots[table], gates[table], returned, carried[micro].shape[0], before
            )
            total = carried[micro].astype(jnp.float32)
            for own_sum in along_first(sums, back=True):
                total = total + own_sum.astype(jnp.float32)
            outputs[step, micro] = total.astype(jnp.bfloat16)
            before = (outputs[step, micro],)
            if step + 1 < segment_count:
                carried[micro] = lax.ppermute(
                    outputs[step, micro],
                    "pipe",
                    [(step, step + 1), (segment_count - 1 - step, segment_count - 2 - step)],
                )

    flags = jnp.stack([(first_step == 0).astype(jnp.int32), down_first.astype(jnp.int32)])
    down_states, up_states = placed_states(
        flags, [outputs[key] for key in turn_order], segment_count, micro_count
    )

    def tangents_of(step, micro):
        turn = step // half
        here = (first_step if turn == 0 else segment_count - 1 - first_step) == step
        first_turn = down_first if turn == 0 else ~down_first
        value = jnp.where(first_turn, key_cotangent[0, 0, micro], key_cotangent[0, 1, micro])
        return jnp.where(here, value, jnp.zeros_like(value))

    tangents = jnp.concatenate([tangents_of(*key) for key in turn_order]).T
    key_grad = summed_grad([normed_rows[key] for key in turn_order], tangents)
    return (down_states[None], up_states[None], key_grad[None])


def solution(mesh):
    return jax.shard_map(
        on_device,
        mesh=mesh,
        in_specs=(
            P(None, "expert", None),
            P(None, "expert", None),
            P("pipe", None),
            P("pipe", "expert", None, None),
            P("pipe", "expert", None, None),
            P("pipe", "expert", None, None),
            P("pipe", None, "expert", None),
            P("pipe", None, "expert", None),
            P("pipe", None, "expert", None),
            P("pipe", None, "expert", None),
            P("pipe", None, None, "expert", None),
        ),
        out_specs=(
            P("pipe", None, "expert", None),
            P("pipe", None, "expert", None),
            P("pipe", "expert", None),
        ),
        check_vma=False,
    )
```

```python
from functools import partial

import jax
import jax.numpy as jnp
from jax import lax
from jax.experimental import pallas as pl
from jax.experimental.pallas import tpu as pltpu
from jax.sharding import PartitionSpec as P

EPSILON = 1e-06
UNTOUCHED = pl.BlockSpec(memory_space=pl.ANY)
SIDE = 4
CAP = 10
TARGETS = 2 * SIDE
MIB = 1 << 20


def device_at(x, y, core):
    return (x % SIDE) * 2 * SIDE + (y % SIDE) * 2 + core


def first_line(shift):
    pairs = []
    for x in range(SIDE):
        for y in range(SIDE):
            pairs.append((device_at(x, y, 0), device_at(x + shift, y, 0)))
            pairs.append((device_at(x, y, 1), device_at(x, y + shift, 1)))
    return pairs


def second_line(shift, flip):
    pairs = []
    for x in range(SIDE):
        for y in range(SIDE):
            pairs.append((device_at(x, y, 0), device_at(x, y + shift, flip)))
            pairs.append((device_at(x, y, 1), device_at(x + shift, y, 1 - flip)))
    return pairs


def backwards(pairs):
    return [(target, source) for source, target in pairs]


HOPS = [(shift, flip) for shift in range(SIDE) for flip in range(2)]


def along_first(blocks, back=False):
    moved = []
    for shift, block in enumerate(blocks):
        pairs = first_line(shift)
        moved.append(
            lax.ppermute(block, "expert", backwards(pairs) if back else pairs) if shift else block
        )
    return moved


def along_second(blocks, back=False):
    moved = []
    for (shift, flip), block in zip(HOPS, blocks):
        pairs = second_line(shift, flip)
        stays = shift == 0 and flip == 0
        moved.append(
            block if stays else lax.ppermute(block, "expert", backwards(pairs) if back else pairs)
        )
    return moved


def normalize_body(carried_ref, scale_ref, out_ref):
    values = carried_ref[...].astype(jnp.float32)
    inv_rms = lax.rsqrt(jnp.mean(values * values, axis=-1, keepdims=True) + EPSILON)
    out_ref[...] = (values * inv_rms * scale_ref[...]).astype(jnp.bfloat16)


def normalize(carried, norm_scale):
    return pl.pallas_call(
        normalize_body,
        name="normalize",
        out_shape=jax.ShapeDtypeStruct(carried.shape, jnp.bfloat16),
        compiler_params=pltpu.CompilerParams(vmem_limit_bytes=8 * MIB),
    )(carried, norm_scale)


def routing_tables(route_ids, route_gates):
    block_count, token_count, pick_count = route_ids.shape
    packed = jnp.concatenate(
        [jnp.swapaxes(route_ids, 1, 2).astype(jnp.float32), jnp.swapaxes(route_gates, 1, 2)], axis=1
    )
    gathered = jnp.concatenate(along_first([packed] * SIDE), axis=-1)
    ids, gates = (gathered[:, :pick_count], gathered[:, pick_count:])
    position = lax.axis_index("expert")
    x, y, core = (position // (2 * SIDE), (position // 2) % SIDE, position % 2)
    shift = jnp.arange(TARGETS, dtype=jnp.int32) // 2
    flip = jnp.arange(TARGETS, dtype=jnp.int32) % 2
    experts = jnp.where(
        core == 0,
        x * 2 * SIDE + ((y + shift) % SIDE) * 2 + flip,
        ((x + shift) % SIDE) * 2 * SIDE + y * 2 + 1 - flip,
    ).astype(jnp.float32)
    matches = (ids[:, None] == experts[None, :, None, None]).astype(jnp.float32)
    chosen = jnp.sum(matches, axis=2)
    gate_of = jnp.sum(matches * gates[:, None], axis=2)
    lane = jnp.arange(SIDE * token_count, dtype=jnp.int32)
    earlier = (lane[:, None] // token_count == lane[None, :] // token_count) & (
        lane[:, None] < lane[None, :]
    )
    rank = jnp.einsum(
        "bet,tu->beu",
        chosen.astype(jnp.bfloat16),
        earlier.astype(jnp.bfloat16),
        preferred_element_type=jnp.float32,
    )
    return jnp.where(chosen > 0, rank, -1.0), gate_of


def slot_pattern(line_count, token_count):
    rows, columns = (line_count * CAP, line_count * token_count)
    row = lax.broadcasted_iota(jnp.int32, (rows, columns), 0)
    column = lax.broadcasted_iota(jnp.int32, (rows, columns), 1)
    return jnp.where(row // CAP == column // token_count, row % CAP, -2).astype(jnp.float32)


def pick_body(slots_ref, *refs):
    row_refs, out_refs = (refs[:SIDE], refs[-TARGETS:])
    token_count = row_refs[0].shape[0]
    pattern = slot_pattern(SIDE, token_count)
    table = jnp.concatenate(
        [(slots_ref[e : e + 1, :] == pattern).astype(jnp.float32) for e in range(TARGETS)], axis=0
    ).astype(jnp.bfloat16)
    rows = jnp.concatenate([ref[...] for ref in row_refs], axis=0)
    picked = jnp.dot(table, rows, preferred_element_type=jnp.float32)
    count = SIDE * CAP
    for e, ref in enumerate(out_refs):
        ref[...] = picked[e * count : (e + 1) * count].astype(jnp.bfloat16)


def pick_rows(slots, rows, after=()):
    token_count, features = rows[0].shape
    block = features
    table_spec = pl.BlockSpec(slots.shape, lambda i: (0, 0))
    out = jax.ShapeDtypeStruct((SIDE * CAP, features), jnp.bfloat16)
    return pl.pallas_call(
        pick_body,
        name="pick_rows",
        grid=(features // block,),
        out_shape=(out,) * TARGETS,
        in_specs=[table_spec]
        + [pl.BlockSpec((token_count, block), lambda i: (0, i))] * SIDE
        + [UNTOUCHED] * len(after),
        out_specs=(pl.BlockSpec((SIDE * CAP, block), lambda i: (0, i)),) * TARGETS,
        compiler_params=pltpu.CompilerParams(vmem_limit_bytes=32 * MIB),
    )(slots, *rows, *after)


def merge_body(slots_ref, gates_ref, *refs):
    row_refs, out_refs = (refs[:TARGETS], refs[-SIDE:])
    token_count = out_refs[0].shape[0]
    pattern = slot_pattern(SIDE, token_count)
    weights = jnp.concatenate(
        [
            jnp.where(slots_ref[e : e + 1, :] == pattern, gates_ref[e : e + 1, :], 0.0)
            for e in range(TARGETS)
        ],
        axis=0,
    )
    rows = jnp.concatenate([ref[...].astype(jnp.float32) for ref in row_refs], axis=0)
    merged = jnp.dot(
        weights.T.astype(jnp.bfloat16),
        rows.astype(jnp.bfloat16),
        preferred_element_type=jnp.float32,
    )
    for m, ref in enumerate(out_refs):
        ref[...] = merged[m * token_count : (m + 1) * token_count].astype(jnp.bfloat16)


def merge_rows(slots, gates, rows, token_count, after=()):
    features = rows[0].shape[1]
    block = features
    table_spec = pl.BlockSpec(slots.shape, lambda i: (0, 0))
    out = jax.ShapeDtypeStruct((token_count, features), jnp.bfloat16)
    return pl.pallas_call(
        merge_body,
        name="merge_rows",
        grid=(features // block,),
        out_shape=(out,) * SIDE,
        in_specs=[table_spec] * 2
        + [pl.BlockSpec((SIDE * CAP, block), lambda i: (0, i))] * TARGETS
        + [UNTOUCHED] * len(after),
        out_specs=(pl.BlockSpec((token_count, block), lambda i: (0, i)),) * SIDE,
        compiler_params=pltpu.CompilerParams(vmem_limit_bytes=32 * MIB),
    )(slots, gates, *rows, *after)


def expert_body(gate_ref, up_ref, down_ref, *refs):
    row_refs, out_refs = (refs[:TARGETS], refs[-TARGETS - 2 : -2])
    rows_scratch, sum_scratch = refs[-2:]
    step = pl.program_id(0)
    count = SIDE * CAP

    @pl.when(step == 0)
    def _():
        rows_scratch[...] = jnp.concatenate(
            [ref[...].astype(jnp.float32) for ref in row_refs], axis=0
        ).astype(jnp.bfloat16)

    rows = rows_scratch[...]
    gate_act = jnp.dot(rows, gate_ref[...], preferred_element_type=jnp.float32)
    up_act = jnp.dot(rows, up_ref[...], preferred_element_type=jnp.float32)
    hidden = (jax.nn.silu(gate_act) * up_act).astype(jnp.bfloat16)
    part = jnp.dot(hidden, down_ref[...], preferred_element_type=jnp.float32)

    @pl.when(step == 0)
    def _():
        sum_scratch[...] = part

    @pl.when(step > 0)
    def _():
        sum_scratch[...] += part

    @pl.when(step == pl.num_programs(0) - 1)
    def _():
        for e, ref in enumerate(out_refs):
            ref[...] = sum_scratch[e * count : (e + 1) * count, :].astype(jnp.bfloat16)


def expert_rows(rows, weights, after=(), block=256):
    gate_mat, up_mat, down_mat = weights
    features, hidden_count = gate_mat.shape
    count = SIDE * CAP
    row_spec = pl.BlockSpec((count, features), lambda i: (0, 0))
    out = jax.ShapeDtypeStruct((count, features), jnp.bfloat16)
    return pl.pallas_call(
        expert_body,
        name="expert_rows",
        grid=(hidden_count // block,),
        out_shape=(out,) * TARGETS,
        in_specs=[
            pl.BlockSpec((features, block), lambda i: (0, i)),
            pl.BlockSpec((features, block), lambda i: (0, i)),
            pl.BlockSpec((block, features), lambda i: (i, 0)),
        ]
        + [row_spec] * TARGETS
        + [UNTOUCHED] * len(after),
        out_specs=(row_spec,) * TARGETS,
        scratch_shapes=[
            pltpu.VMEM((TARGETS * count, features), jnp.bfloat16),
            pltpu.VMEM((TARGETS * count, features), jnp.float32),
        ],
        compiler_params=pltpu.CompilerParams(vmem_limit_bytes=50 * MIB),
    )(gate_mat, up_mat, down_mat, *rows, *after)


def grad_body(tangents_ref, *refs):
    row_refs, out_ref = (refs[:-1], refs[-1])
    rows = jnp.concatenate([ref[...] for ref in row_refs], axis=0)
    grad = jnp.dot(tangents_ref[...], rows, preferred_element_type=jnp.float32)
    own_rows = out_ref.shape[2]
    for e in range(out_ref.shape[0]):
        out_ref[e] = grad[:, e * own_rows : (e + 1) * own_rows].astype(jnp.bfloat16)


def summed_grad(normed_rows, tangents):
    expert_count = lax.axis_size("expert")
    own_rows = normed_rows[0].shape[1] // expert_count
    partial_grad = pl.pallas_call(
        grad_body,
        name="key_grad",
        out_shape=jax.ShapeDtypeStruct((expert_count, tangents.shape[0], own_rows), jnp.bfloat16),
        compiler_params=pltpu.CompilerParams(vmem_limit_bytes=32 * MIB),
    )(tangents, *normed_rows)
    gathered = lax.all_to_all(partial_grad, "expert", split_axis=0, concat_axis=0, tiled=True)
    return jnp.sum(gathered.astype(jnp.float32), axis=0).T


def on_device(
    down_tokens,
    up_tokens,
    norm_gain,
    w_gate,
    w_up,
    w_down,
    down_ids,
    down_gates,
    up_ids,
    up_gates,
    key_cotangent,
):
    segment_count = lax.axis_size("pipe")
    segment_pos = lax.axis_index("pipe")
    micro_count = down_tokens.shape[0]
    norm_scale = norm_gain
    weights = (w_gate[0, 0], w_up[0, 0], w_down[0, 0])
    down_first = segment_pos < segment_count // 2
    first_step = jnp.minimum(segment_pos, segment_count - 1 - segment_pos)
    half = segment_count // 2
    carried = [
        jnp.where(segment_pos == 0, down_tokens[micro], up_tokens[micro])
        for micro in range(micro_count)
    ]
    route_ids = jnp.concatenate(
        [jnp.where(down_first, down_ids[0], up_ids[0]), jnp.where(down_first, up_ids[0], down_ids[0])]
    )
    route_gates = jnp.concatenate(
        [
            jnp.where(down_first, down_gates[0], up_gates[0]),
            jnp.where(down_first, up_gates[0], down_gates[0]),
        ]
    )
    normed = normalize(carried[0], norm_scale)
    route_ids, route_gates, normed = lax.optimization_barrier((route_ids, route_gates, normed))
    slots, gates = routing_tables(route_ids, route_gates)
    turn_order = [(step, micro) for step in range(segment_count) for micro in range(micro_count)]
    outputs = {}
    normed_rows = {}
    for step in range(segment_count):
        picked = {}
        for micro in range(micro_count):
            if (step, micro) != (0, 0):
                normed = normalize(carried[micro], norm_scale)
            normed_rows[step, micro] = normed
            table = step // half * micro_count + micro
            before = (picked[micro - 1][0],) if micro else ()
            picked[micro] = pick_rows(slots[table], along_first([normed] * SIDE), before)
        finished = {}
        before = (picked[micro_count - 1][0],)
        for micro in range(micro_count):
            finished[micro] = expert_rows(along_second(picked[micro]), weights, before)
            before = (finished[micro][0],)
        for micro in range(micro_count):
            table = step // half * micro_count + micro
            returned = along_second(finished[micro], back=True)
            sums = merge_rows(
                slots[table], gates[table], returned, carried[micro].shape[0], before
            )
            before = (sums[0],)
            total = carried[micro].astype(jnp.float32)
            for own_sum in along_first(sums, back=True):
                total = total + own_sum.astype(jnp.float32)
            outputs[step, micro] = total.astype(jnp.bfloat16)
            if step + 1 < segment_count:
                carried[micro] = lax.ppermute(
                    outputs[step, micro],
                    "pipe",
                    [(step, step + 1), (segment_count - 1 - step, segment_count - 2 - step)],
                )

    def turns(values):
        chosen = []
        for turn in range(2):
            for micro in range(micro_count):
                value = values[turn * half, micro]
                for offset in range(1, half):
                    step = turn * half + offset
                    here = (first_step if turn == 0 else segment_count - 1 - first_step) == step
                    value = jnp.where(here, values[step, micro], value)
                chosen.append(value)
        return chosen

    turn_outputs = turns(outputs)
    first, second = (jnp.stack(turn_outputs[:micro_count]), jnp.stack(turn_outputs[micro_count:]))
    down_states = jnp.where(down_first, first, second)
    up_states = jnp.where(down_first, second, first)
    def tangents_of(step, micro):
        turn = step // half
        here = (first_step if turn == 0 else segment_count - 1 - first_step) == step
        first_turn = down_first if turn == 0 else ~down_first
        value = jnp.where(first_turn, key_cotangent[0, 0, micro], key_cotangent[0, 1, micro])
        return jnp.where(here, value, jnp.zeros_like(value))

    tangents = jnp.concatenate([tangents_of(*key) for key in turn_order]).T
    key_grad = summed_grad([normed_rows[key] for key in turn_order], tangents)
    return (down_states[None], up_states[None], key_grad[None])


def solution(mesh):
    return jax.shard_map(
        on_device,
        mesh=mesh,
        in_specs=(
            P(None, "expert", None),
            P(None, "expert", None),
            P("pipe", None),
            P("pipe", "expert", None, None),
            P("pipe", "expert", None, None),
            P("pipe", "expert", None, None),
            P("pipe", None, "expert", None),
            P("pipe", None, "expert", None),
            P("pipe", None, "expert", None),
            P("pipe", None, "expert", None),
            P("pipe", None, None, "expert", None),
        ),
        out_specs=(
            P("pipe", None, "expert", None),
            P("pipe", None, "expert", None),
            P("pipe", "expert", None),
        ),
        check_vma=False,
    )
```

```python
from functools import partial

import jax
import jax.numpy as jnp
from jax import lax
from jax.experimental import pallas as pl
from jax.experimental.pallas import tpu as pltpu
from jax.sharding import PartitionSpec as P

EPSILON = 1e-06
UNTOUCHED = pl.BlockSpec(memory_space=pl.ANY)
SIDE = 4
CAP = 10
TARGETS = 2 * SIDE
MIB = 1 << 20


def device_at(x, y, core):
    return (x % SIDE) * 2 * SIDE + (y % SIDE) * 2 + core


def first_line(shift):
    pairs = []
    for x in range(SIDE):
        for y in range(SIDE):
            pairs.append((device_at(x, y, 0), device_at(x + shift, y, 0)))
            pairs.append((device_at(x, y, 1), device_at(x, y + shift, 1)))
    return pairs


def second_line(shift, flip):
    pairs = []
    for x in range(SIDE):
        for y in range(SIDE):
            pairs.append((device_at(x, y, 0), device_at(x, y + shift, flip)))
            pairs.append((device_at(x, y, 1), device_at(x + shift, y, 1 - flip)))
    return pairs


def backwards(pairs):
    return [(target, source) for source, target in pairs]


HOPS = [(shift, flip) for shift in range(SIDE) for flip in range(2)]


def along_first(blocks, back=False):
    moved = []
    for shift, block in enumerate(blocks):
        pairs = first_line(shift)
        moved.append(
            lax.ppermute(block, "expert", backwards(pairs) if back else pairs) if shift else block
        )
    return moved


def along_second(blocks, back=False):
    moved = []
    for (shift, flip), block in zip(HOPS, blocks):
        pairs = second_line(shift, flip)
        stays = shift == 0 and flip == 0
        moved.append(
            block if stays else lax.ppermute(block, "expert", backwards(pairs) if back else pairs)
        )
    return moved


def normalize_body(carried_ref, scale_ref, out_ref):
    values = carried_ref[...].astype(jnp.float32)
    inv_rms = lax.rsqrt(jnp.mean(values * values, axis=-1, keepdims=True) + EPSILON)
    out_ref[...] = (values * inv_rms * scale_ref[...]).astype(jnp.bfloat16)


def normalize(carried, norm_scale):
    return pl.pallas_call(
        normalize_body,
        name="normalize",
        out_shape=jax.ShapeDtypeStruct(carried.shape, jnp.bfloat16),
        compiler_params=pltpu.CompilerParams(vmem_limit_bytes=8 * MIB),
    )(carried, norm_scale)


def routing_tables(route_ids, route_gates):
    block_count, token_count, pick_count = route_ids.shape
    packed = jnp.concatenate(
        [jnp.swapaxes(route_ids, 1, 2).astype(jnp.float32), jnp.swapaxes(route_gates, 1, 2)], axis=1
    )
    gathered = jnp.concatenate(along_first([packed] * SIDE), axis=-1)
    ids, gates = (gathered[:, :pick_count], gathered[:, pick_count:])
    position = lax.axis_index("expert")
    x, y, core = (position // (2 * SIDE), (position // 2) % SIDE, position % 2)
    shift = jnp.arange(TARGETS, dtype=jnp.int32) // 2
    flip = jnp.arange(TARGETS, dtype=jnp.int32) % 2
    experts = jnp.where(
        core == 0,
        x * 2 * SIDE + ((y + shift) % SIDE) * 2 + flip,
        ((x + shift) % SIDE) * 2 * SIDE + y * 2 + 1 - flip,
    ).astype(jnp.float32)
    matches = (ids[:, None] == experts[None, :, None, None]).astype(jnp.float32)
    chosen = jnp.sum(matches, axis=2)
    gate_of = jnp.sum(matches * gates[:, None], axis=2)
    lane = jnp.arange(SIDE * token_count, dtype=jnp.int32)
    earlier = (lane[:, None] // token_count == lane[None, :] // token_count) & (
        lane[:, None] < lane[None, :]
    )
    rank = jnp.einsum(
        "bet,tu->beu",
        chosen.astype(jnp.bfloat16),
        earlier.astype(jnp.bfloat16),
        preferred_element_type=jnp.float32,
    )
    return jnp.where(chosen > 0, rank, -1.0), gate_of


def slot_pattern(line_count, token_count):
    rows, columns = (line_count * CAP, line_count * token_count)
    row = lax.broadcasted_iota(jnp.int32, (rows, columns), 0)
    column = lax.broadcasted_iota(jnp.int32, (rows, columns), 1)
    return jnp.where(row // CAP == column // token_count, row % CAP, -2).astype(jnp.float32)


def pick_body(slots_ref, *refs):
    row_refs, out_refs = (refs[:SIDE], refs[-TARGETS:])
    token_count = row_refs[0].shape[0]
    pattern = slot_pattern(SIDE, token_count)
    table = jnp.concatenate(
        [(slots_ref[e : e + 1, :] == pattern).astype(jnp.float32) for e in range(TARGETS)], axis=0
    ).astype(jnp.bfloat16)
    rows = jnp.concatenate([ref[...] for ref in row_refs], axis=0)
    picked = jnp.dot(table, rows, preferred_element_type=jnp.float32)
    count = SIDE * CAP
    for e, ref in enumerate(out_refs):
        ref[...] = picked[e * count : (e + 1) * count].astype(jnp.bfloat16)


def pick_rows(slots, rows, after=()):
    token_count, features = rows[0].shape
    block = features
    table_spec = pl.BlockSpec(slots.shape, lambda i: (0, 0))
    out = jax.ShapeDtypeStruct((SIDE * CAP, features), jnp.bfloat16)
    return pl.pallas_call(
        pick_body,
        name="pick_rows",
        grid=(features // block,),
        out_shape=(out,) * TARGETS,
        in_specs=[table_spec]
        + [pl.BlockSpec((token_count, block), lambda i: (0, i))] * SIDE
        + [UNTOUCHED] * len(after),
        out_specs=(pl.BlockSpec((SIDE * CAP, block), lambda i: (0, i)),) * TARGETS,
        compiler_params=pltpu.CompilerParams(vmem_limit_bytes=20 * MIB),
    )(slots, *rows, *after)


def merge_body(slots_ref, gates_ref, *refs):
    row_refs, out_refs = (refs[:TARGETS], refs[-SIDE:])
    token_count = out_refs[0].shape[0]
    pattern = slot_pattern(SIDE, token_count)
    weights = jnp.concatenate(
        [
            jnp.where(slots_ref[e : e + 1, :] == pattern, gates_ref[e : e + 1, :], 0.0)
            for e in range(TARGETS)
        ],
        axis=0,
    )
    rows = jnp.concatenate([ref[...].astype(jnp.float32) for ref in row_refs], axis=0)
    merged = jnp.dot(
        weights.T.astype(jnp.bfloat16),
        rows.astype(jnp.bfloat16),
        preferred_element_type=jnp.float32,
    )
    for m, ref in enumerate(out_refs):
        ref[...] = merged[m * token_count : (m + 1) * token_count].astype(jnp.bfloat16)


def merge_rows(slots, gates, rows, token_count, after=()):
    features = rows[0].shape[1]
    block = features
    table_spec = pl.BlockSpec(slots.shape, lambda i: (0, 0))
    out = jax.ShapeDtypeStruct((token_count, features), jnp.bfloat16)
    return pl.pallas_call(
        merge_body,
        name="merge_rows",
        grid=(features // block,),
        out_shape=(out,) * SIDE,
        in_specs=[table_spec] * 2
        + [pl.BlockSpec((SIDE * CAP, block), lambda i: (0, i))] * TARGETS
        + [UNTOUCHED] * len(after),
        out_specs=(pl.BlockSpec((token_count, block), lambda i: (0, i)),) * SIDE,
        compiler_params=pltpu.CompilerParams(vmem_limit_bytes=20 * MIB),
    )(slots, gates, *rows, *after)


def expert_body(gate_ref, up_ref, down_ref, *refs):
    row_refs, out_refs = (refs[:TARGETS], refs[-TARGETS - 2 : -2])
    rows_scratch, sum_scratch = refs[-2:]
    step = pl.program_id(0)
    count = SIDE * CAP

    @pl.when(step == 0)
    def _():
        rows_scratch[...] = jnp.concatenate(
            [ref[...].astype(jnp.float32) for ref in row_refs], axis=0
        ).astype(jnp.bfloat16)

    rows = rows_scratch[...]
    gate_act = jnp.dot(rows, gate_ref[...], preferred_element_type=jnp.float32)
    up_act = jnp.dot(rows, up_ref[...], preferred_element_type=jnp.float32)
    hidden = (jax.nn.silu(gate_act) * up_act).astype(jnp.bfloat16)
    part = jnp.dot(hidden, down_ref[...], preferred_element_type=jnp.float32)

    @pl.when(step == 0)
    def _():
        sum_scratch[...] = part

    @pl.when(step > 0)
    def _():
        sum_scratch[...] += part

    @pl.when(step == pl.num_programs(0) - 1)
    def _():
        for e, ref in enumerate(out_refs):
            ref[...] = sum_scratch[e * count : (e + 1) * count, :].astype(jnp.bfloat16)


def expert_rows(rows, weights, after=(), block=256):
    gate_mat, up_mat, down_mat = weights
    features, hidden_count = gate_mat.shape
    count = SIDE * CAP
    row_spec = pl.BlockSpec((count, features), lambda i: (0, 0))
    out = jax.ShapeDtypeStruct((count, features), jnp.bfloat16)
    return pl.pallas_call(
        expert_body,
        name="expert_rows",
        grid=(hidden_count // block,),
        out_shape=(out,) * TARGETS,
        in_specs=[
            pl.BlockSpec((features, block), lambda i: (0, i)),
            pl.BlockSpec((features, block), lambda i: (0, i)),
            pl.BlockSpec((block, features), lambda i: (i, 0)),
        ]
        + [row_spec] * TARGETS
        + [UNTOUCHED] * len(after),
        out_specs=(row_spec,) * TARGETS,
        scratch_shapes=[
            pltpu.VMEM((TARGETS * count, features), jnp.bfloat16),
            pltpu.VMEM((TARGETS * count, features), jnp.float32),
        ],
        compiler_params=pltpu.CompilerParams(vmem_limit_bytes=40 * MIB),
    )(gate_mat, up_mat, down_mat, *rows, *after)


def grad_body(tangents_ref, *refs):
    row_refs, out_ref = (refs[:-1], refs[-1])
    rows = jnp.concatenate([ref[...] for ref in row_refs], axis=0)
    grad = jnp.dot(tangents_ref[...], rows, preferred_element_type=jnp.float32)
    own_rows = out_ref.shape[2]
    for e in range(out_ref.shape[0]):
        out_ref[e] = grad[:, e * own_rows : (e + 1) * own_rows].astype(jnp.bfloat16)


def summed_grad(normed_rows, tangents):
    expert_count = lax.axis_size("expert")
    own_rows = normed_rows[0].shape[1] // expert_count
    partial_grad = pl.pallas_call(
        grad_body,
        name="key_grad",
        out_shape=jax.ShapeDtypeStruct((expert_count, tangents.shape[0], own_rows), jnp.bfloat16),
        compiler_params=pltpu.CompilerParams(vmem_limit_bytes=20 * MIB),
    )(tangents, *normed_rows)
    gathered = lax.all_to_all(partial_grad, "expert", split_axis=0, concat_axis=0, tiled=True)
    return jnp.sum(gathered.astype(jnp.float32), axis=0).T


def on_device(
    down_tokens,
    up_tokens,
    norm_gain,
    w_gate,
    w_up,
    w_down,
    down_ids,
    down_gates,
    up_ids,
    up_gates,
    key_cotangent,
):
    segment_count = lax.axis_size("pipe")
    segment_pos = lax.axis_index("pipe")
    micro_count = down_tokens.shape[0]
    norm_scale = norm_gain
    weights = (w_gate[0, 0], w_up[0, 0], w_down[0, 0])
    down_first = segment_pos < segment_count // 2
    first_step = jnp.minimum(segment_pos, segment_count - 1 - segment_pos)
    half = segment_count // 2
    carried = [
        jnp.where(segment_pos == 0, down_tokens[micro], up_tokens[micro])
        for micro in range(micro_count)
    ]
    route_ids = jnp.concatenate(
        [jnp.where(down_first, down_ids[0], up_ids[0]), jnp.where(down_first, up_ids[0], down_ids[0])]
    )
    route_gates = jnp.concatenate(
        [
            jnp.where(down_first, down_gates[0], up_gates[0]),
            jnp.where(down_first, up_gates[0], down_gates[0]),
        ]
    )
    normed = normalize(carried[0], norm_scale)
    slots, gates = routing_tables(route_ids, route_gates)
    turn_order = [(step, micro) for step in range(segment_count) for micro in range(micro_count)]
    outputs = {}
    normed_rows = {}
    for step in range(segment_count):
        picked = {}
        for micro in range(micro_count):
            if (step, micro) != (0, 0):
                normed = normalize(carried[micro], norm_scale)
            normed_rows[step, micro] = normed
            table = step // half * micro_count + micro
            before = (picked[micro - 1][0],) if micro else ()
            picked[micro] = pick_rows(slots[table], along_first([normed] * SIDE), before)
        finished = {}
        before = (picked[micro_count - 1][0],)
        for micro in range(micro_count):
            finished[micro] = expert_rows(along_second(picked[micro]), weights, before)
            before = (finished[micro][0],)
        for micro in range(micro_count):
            table = step // half * micro_count + micro
            returned = along_second(finished[micro], back=True)
            sums = merge_rows(
                slots[table], gates[table], returned, carried[micro].shape[0], before
            )
            before = (sums[0],)
            total = carried[micro].astype(jnp.float32)
            for own_sum in along_first(sums, back=True):
                total = total + own_sum.astype(jnp.float32)
            outputs[step, micro] = total.astype(jnp.bfloat16)
            if step + 1 < segment_count:
                carried[micro] = lax.ppermute(
                    outputs[step, micro],
                    "pipe",
                    [(step, step + 1), (segment_count - 1 - step, segment_count - 2 - step)],
                )

    early = [key for key in turn_order if key[0] < half]
    held = lax.optimization_barrier(([outputs[key] for key in early], sums[0]))
    outputs.update(zip(early, held[0]))

    def turns(values):
        chosen = []
        for turn in range(2):
            for micro in range(micro_count):
                value = values[turn * half, micro]
                for offset in range(1, half):
                    step = turn * half + offset
                    here = (first_step if turn == 0 else segment_count - 1 - first_step) == step
                    value = jnp.where(here, values[step, micro], value)
                chosen.append(value)
        return chosen

    turn_outputs = turns(outputs)
    first, second = (jnp.stack(turn_outputs[:micro_count]), jnp.stack(turn_outputs[micro_count:]))
    down_states = jnp.where(down_first, first, second)
    up_states = jnp.where(down_first, second, first)
    def tangents_of(step, micro):
        turn = step // half
        here = (first_step if turn == 0 else segment_count - 1 - first_step) == step
        first_turn = down_first if turn == 0 else ~down_first
        value = jnp.where(first_turn, key_cotangent[0, 0, micro], key_cotangent[0, 1, micro])
        return jnp.where(here, value, jnp.zeros_like(value))

    tangents = jnp.concatenate([tangents_of(*key) for key in turn_order]).T
    key_grad = summed_grad([normed_rows[key] for key in turn_order], tangents)
    return (down_states[None], up_states[None], key_grad[None])


def solution(mesh):
    return jax.shard_map(
        on_device,
        mesh=mesh,
        in_specs=(
            P(None, "expert", None),
            P(None, "expert", None),
            P("pipe", None),
            P("pipe", "expert", None, None),
            P("pipe", "expert", None, None),
            P("pipe", "expert", None, None),
            P("pipe", None, "expert", None),
            P("pipe", None, "expert", None),
            P("pipe", None, "expert", None),
            P("pipe", None, "expert", None),
            P("pipe", None, None, "expert", None),
        ),
        out_specs=(
            P("pipe", None, "expert", None),
            P("pipe", None, "expert", None),
            P("pipe", "expert", None),
        ),
        check_vma=False,
    )
```
